512 devices in a mesh: dp: 32 (over x, z), tensor: 16 (over y, core).
Axes of the slice: x: 4, y: 8, z: 8, core: 2. Of those that a mesh axis runs over, the one named last changes fastest.
Arguments:
- tokens: bfloat16 [8192, 4096], P('dp', 'tensor'), may hold values from -6 to 6
- out_grad: bfloat16 [8192, 4096], P('dp', 'tensor'), may hold values from -0.59765625 to 0.59765625
- w_in: bfloat16 [384, 128, 128], P('tensor'), may hold values from -0.25 to 0.25
- w_out: bfloat16 [384, 128, 128], P('tensor'), may hold values from -0.25 to 0.25
- block_rows: int32 [16, 24], P('tensor'), may hold values from -1 to 31, as said below
- block_cols: int32 [16, 24], P('tensor'), may hold values from -1 to 6, as said below
Outputs:
- in_grad: bfloat16 [8192, 4096], P('dp')
- win_grad: float32 [384, 16384], P('tensor', 'dp')
- wout_grad: float32 [384, 16384], P('tensor', 'dp')
The draws below stay inside these ranges and needn't reach their ends.
Inputs may be any that keep to these rules, and one draw needn't show every extreme that they name: `block_rows`: -1 marks an empty slot; the live slots of one tensor index name distinct blocks; at least 12 slots of each tensor index are live, and all 24 slots of some tensor index are live. `block_cols`: -1 exactly where block_rows is -1.
All inputs are finite; a program needn't handle non-finite values.
Results may differ from the reference program's by a relative error of at most 0.02.
Values may be sent and summed in bfloat16 or wider, within the bound.
No kernel may reach another device: no remote copies, remote signals or barrier semaphores. Data moves between devices by JAX's collectives and lax.ppermute only.
A program may use at most 64 MiB of HBM per device.

```python
import jax
import jax.numpy as jnp
from jax import lax

D = 4096
BLK = 128
TOK_DEV = 256
CAP = 24
TOKENS = 8192
ROWBLK = 32
HID_DEV = 7
SLOTS = 384
N_DP = 32
N_TENSOR = 16


def shared_layout(key):
    base = jax.random.fold_in(key, 7)
    key_full, key_count, key_place, key_order = jax.random.split(base, 4)
    full_index = jax.random.randint(key_full, (), 0, N_TENSOR)
    counts = jax.random.randint(key_count, (N_TENSOR,), CAP // 2, CAP + 1)
    counts = jnp.where(jnp.arange(N_TENSOR) == full_index, CAP, counts)
    place_keys = jax.random.split(key_place, N_TENSOR)
    order_keys = jax.random.split(key_order, N_TENSOR)
    places = jax.vmap(lambda k: jax.random.permutation(k, ROWBLK * HID_DEV)[:CAP])(place_keys)
    ranks = jax.vmap(lambda k: jax.random.permutation(k, CAP))(order_keys)
    live = ranks < counts[:, None]
    rows = jnp.where(live, places // HID_DEV, -1).astype(jnp.int32)
    cols = jnp.where(live, places % HID_DEV, -1).astype(jnp.int32)
    return (rows, cols)


def draw_block_rows(key, part):
    return shared_layout(key)[0]


def draw_block_cols(key, part):
    return shared_layout(key)[1]


def level_of(rng, extent, cuts, low, high):
    factor_of = 1.0
    for dim, blocks in cuts:
        draws = jax.random.uniform(jax.random.fold_in(jax.random.fold_in(rng, 6), dim), (blocks,), jnp.float32, low / len(cuts), high / len(cuts))
        factor_of = factor_of * jnp.repeat(jnp.exp(draws), extent[dim] // blocks).reshape((-1,) + (1,) * (len(extent) - 1 - dim))
    return factor_of


def noise(rng, shape, width, reach, shards=(), kind=jnp.bfloat16):
    values = jax.random.normal(rng, shape, jnp.float32) * width
    if len(shards) > 0:
        values = level_of(rng, shape, shards, -0.22, 0.18) * values
    return jnp.clip(values, min=-reach, max=reach).astype(kind)


def setup_inputs(seed: int = 0) -> dict:
    keys = jax.random.split(jax.random.key(seed), 7)
    return {
        "tokens": noise(keys[0], (TOKENS, D), 1.0, 6.0, ((0, 32), (1, 16))),
        "out_grad": noise(keys[1], (TOKENS, D), 0.1, 0.59765625, ((0, 32), (1, 16))),
        "w_in": noise(keys[2], (SLOTS, BLK, BLK), (4 * BLK) ** -0.5, 0.25, ((0, 16),)),
        "w_out": noise(keys[3], (SLOTS, BLK, BLK), (4 * BLK) ** -0.5, 0.25, ((0, 16),)),
        "block_rows": draw_block_rows(jax.random.fold_in(keys[6], 71), 0),
        "block_cols": draw_block_cols(jax.random.fold_in(keys[6], 71), 0),
    }


highest = lax.Precision.HIGHEST
clip_limit = 4.0


def device_pass(tokens_now, cotangent, w_in, w_out, block_rows, block_cols, bin_scale):
    rows = block_rows.reshape(-1)
    cols = block_cols.reshape(-1)
    live = rows >= 0
    livef = live.astype(jnp.float32)
    shard_of = (jnp.arange(rows.shape[0], dtype=jnp.int32) // CAP).astype(jnp.int32)
    global_col = jnp.where(live, shard_of * HID_DEV + cols, 0).astype(jnp.int32)
    safe_rows = jnp.where(live, rows, 0).astype(jnp.int32)
    col_hot = (global_col[:, None] == jnp.arange(HID_DEV * N_TENSOR, dtype=jnp.int32)[None, :]).astype(jnp.float32) * livef[:, None]
    row_hot = (safe_rows[:, None] == jnp.arange(ROWBLK, dtype=jnp.int32)[None, :]).astype(jnp.float32) * livef[:, None]
    in_blocks = tokens_now.reshape(TOK_DEV, ROWBLK, BLK).transpose(1, 0, 2)
    grad_blocks = cotangent.reshape(TOK_DEV, ROWBLK, BLK).transpose(1, 0, 2)
    picked = jnp.take(in_blocks, safe_rows, axis=0).astype(jnp.float32)
    picked_grad = jnp.take(grad_blocks, safe_rows, axis=0).astype(jnp.float32)
    win_wide = w_in.astype(jnp.float32)
    wout_wide = w_out.astype(jnp.float32)
    pre = jnp.einsum('sc,sth->cth', col_hot, jnp.einsum('stk,skh->sth', picked, win_wide), precision=highest)
    hidden = jax.nn.silu(pre).astype(jnp.bfloat16)
    dhidden = jnp.einsum('sc,sth->cth', col_hot, jnp.einsum('std,shd->sth', picked_grad, wout_wide), precision=highest)
    sigma = jax.nn.sigmoid(pre)
    dpre = (dhidden * sigma * (1.0 + pre * (1.0 - sigma))).astype(jnp.bfloat16)
    dpre_picked = jnp.take(dpre, global_col, axis=0).astype(jnp.float32)
    hidden_picked = jnp.take(hidden, global_col, axis=0).astype(jnp.float32)
    slot_terms = jnp.einsum('sth,sdh->std', dpre_picked, win_wide)

    def shard_part(total, index):
        hot_now = lax.dynamic_slice_in_dim(row_hot, index * CAP, CAP, 0)
        terms_now = lax.dynamic_slice_in_dim(slot_terms, index * CAP, CAP, 0)
        part = jnp.einsum('sr,std->rtd', hot_now, terms_now, precision=highest)
        part = lax.optimization_barrier(part.astype(jnp.bfloat16))
        return total + part.astype(jnp.float32), None

    zero_grad = jnp.zeros((ROWBLK, TOK_DEV, BLK), jnp.float32)
    in_grad, unused = lax.scan(shard_part, zero_grad, jnp.arange(N_TENSOR, dtype=jnp.int32))
    in_grad = in_grad.transpose(1, 0, 2).reshape(TOK_DEV, D).astype(jnp.bfloat16)
    grad_in = jnp.einsum('stk,sth->skh', picked, dpre_picked) * livef[:, None, None]
    grad_out = jnp.einsum('sth,std->shd', hidden_picked, picked_grad) * livef[:, None, None]
    bins_in = jnp.floor(jnp.clip(grad_in, -clip_limit, clip_limit) * bin_scale)
    bins_out = jnp.floor(jnp.clip(grad_out, -clip_limit, clip_limit) * bin_scale)
    return in_grad, bins_in, bins_out


def reference(tokens, out_grad, w_in, w_out, block_rows, block_cols):
    bin_scale = 4194304.0 / N_DP
    token_sets = tokens.reshape(N_DP, TOK_DEV, D)
    grad_sets = out_grad.reshape(N_DP, TOK_DEV, D)

    def advance(carry, pair):
        in_grad, bins_in, bins_out = device_pass(pair[0], pair[1], w_in, w_out, block_rows, block_cols, bin_scale)
        return (carry[0] + bins_in, carry[1] + bins_out), in_grad

    zeros = jnp.zeros((N_TENSOR * CAP, BLK, BLK), jnp.float32)
    (total_in, total_out), grads = lax.scan(advance, (zeros, zeros), (token_sets, grad_sets))
    in_grad = grads.reshape(TOKENS, D)
    win_grad = (total_in / bin_scale).reshape(N_TENSOR * CAP, BLK * BLK)
    wout_grad = (total_out / bin_scale).reshape(N_TENSOR * CAP, BLK * BLK)
    return in_grad, win_grad, wout_grad
```

```python
import jax
import jax.numpy as jnp
from jax import lax
from jax.experimental import pallas as pl
from jax.experimental.pallas import tpu as pltpu
from jax.sharding import PartitionSpec as P

FF = 14336
CLIP = 4.0
LANES = 128
BF = jnp.bfloat16
F32 = jnp.float32
VMEM_LIMIT = 50 * 1024 * 1024


def dot(a, b, ca, cb):
    return lax.dot_general(a, b, (((ca,), (cb,)), ((), ())), preferred_element_type=F32)


def slot_index(rows_ref, cols_ref, s, dead_col):
    row = rows_ref[0, s]
    live = row >= 0
    return jnp.where(live, row, 0), jnp.where(live, cols_ref[0, s], dead_col)


def pack_kernel(tok_ref, grad_ref, out_ref):
    for b in range(out_ref.shape[0]):
        out_ref[b, 0] = tok_ref[:, b * LANES : (b + 1) * LANES]
        out_ref[b, 1] = grad_ref[:, b * LANES : (b + 1) * LANES]


def bins_kernel(bin_scale, groups, rows_ref, cols_ref, act_ref, win_ref, wout_ref, bins_ref, dpre_ref,
                pre_ref, dh_ref, hid_ref, wide_ref):
    slots = win_ref.shape[0]
    col_count = pre_ref.shape[0] - 1
    per = LANES // groups
    pre_ref[...] = jnp.zeros_like(pre_ref)
    dh_ref[...] = jnp.zeros_like(dh_ref)
    index = [slot_index(rows_ref, cols_ref, s, col_count) for s in range(slots)]
    for s in range(slots):
        r, c = index[s]
        pre_ref[c] += dot(act_ref[r, 0], win_ref[s], 1, 0)
        dh_ref[c] += dot(act_ref[r, 1], wout_ref[s], 1, 1)
    for c in range(col_count):
        pre = pre_ref[c]
        sigma = jax.nn.sigmoid(pre)
        hid_ref[c] = (pre * sigma).astype(BF)
        dpre_ref[c] = (dh_ref[c] * sigma * (1.0 + pre * (1.0 - sigma))).astype(BF)
    hid_ref[col_count] = jnp.zeros(hid_ref.shape[1:], BF)
    dpre_ref[col_count] = jnp.zeros(dpre_ref.shape[1:], BF)

    def put(val, slot):
        val = jnp.floor(jnp.clip(val, -CLIP, CLIP) * bin_scale)
        for g in range(groups):
            wide_ref[g, slot * per : (slot + 1) * per, :] = val[g * per : (g + 1) * per]

    for s in range(slots):
        r, c = index[s]
        put(dot(act_ref[r, 0], dpre_ref[c], 0, 0), s)
        put(dot(hid_ref[c], act_ref[r, 1], 0, 0), slots + s)
    for g in range(groups):
        bins_ref[g] = wide_ref[g].astype(BF)


def back_kernel(rows_ref, cols_ref, dpre_ref, win_ref, keep_ref, send_ref, acc_ref):
    slots = win_ref.shape[0]
    col_count = dpre_ref.shape[0] - 1
    half = keep_ref.shape[0]
    core = lax.rem(lax.axis_index("tensor"), 2)
    acc_ref[...] = jnp.zeros_like(acc_ref)
    for s in range(slots):
        r, c = slot_index(rows_ref, cols_ref, s, col_count)
        acc_ref[r] += dot(dpre_ref[c], win_ref[s], 1, 1)
    mine = pl.multiple_of(core * half, half)
    other = pl.multiple_of((1 - core) * half, half)
    for b in range(acc_ref.shape[0]):
        at = slice(b * LANES, (b + 1) * LANES)
        keep_ref[:, at] = acc_ref[b, pl.ds(mine, half), :].astype(BF)
        send_ref[:, at] = acc_ref[b, pl.ds(other, half), :].astype(BF)


def spread_kernel(in_ref, out_ref):
    total = in_ref[0].astype(F32)
    for k in range(1, in_ref.shape[0]):
        total += in_ref[k].astype(F32)
    total = total.astype(BF)
    for k in range(out_ref.shape[0]):
        out_ref[k] = total


def join_kernel(mine_ref, other_ref, out_ref, sems):
    half = mine_ref.shape[0]
    core = lax.rem(lax.axis_index("tensor"), 2)
    a = pltpu.make_async_copy(mine_ref, out_ref.at[pl.ds(pl.multiple_of(core * half, half), half)], sems.at[0])
    b = pltpu.make_async_copy(other_ref, out_ref.at[pl.ds(pl.multiple_of((1 - core) * half, half), half)], sems.at[1])
    a.start()
    b.start()
    a.wait()
    b.wait()


def finish_kernel(bin_scale, in_ref, win_ref, wout_ref, wide_ref):
    slots = win_ref.shape[0]
    per = in_ref.shape[0] // (2 * slots)
    wide_ref[...] = in_ref[...].astype(F32) / bin_scale
    for j in range(per):
        at = slice(j * LANES, (j + 1) * LANES)
        win_ref[:, at] = wide_ref[pl.ds(j, slots, stride=per), :]
        wout_ref[:, at] = wide_ref[pl.ds(slots * per + j, slots, stride=per), :]


def vm():
    return pl.BlockSpec(memory_space=pltpu.VMEM)


def sm():
    return pl.BlockSpec(memory_space=pltpu.SMEM)


def hbm():
    return pl.BlockSpec(memory_space=pl.ANY)


def sds(shape, dtype):
    return jax.ShapeDtypeStruct(shape, dtype)


def params():
    return pltpu.CompilerParams(vmem_limit_bytes=VMEM_LIMIT)


def cost(flops, nbytes):
    return pl.CostEstimate(flops=flops, bytes_accessed=nbytes, transcendentals=0)


def make_local(z_size):
    def local(tokens, out_grad, w_in, w_out, block_rows, block_cols):
        n_dp = lax.axis_size("dp")
        n_t = lax.axis_size("tensor")
        bin_scale = 4194304.0 / n_dp
        tok, feat = tokens.shape
        slots, side, _ = w_in.shape
        own_blocks = feat // side
        blocks = own_blocks * n_t
        col_count = FF // side // n_t
        ny = n_t // 2
        x_size = n_dp // z_size
        half = tok // 2
        y_groups = [[2 * i + c for i in range(ny)] for c in range(2)]
        z_groups = [[z_size * i + j for j in range(z_size)] for i in range(x_size)]
        x_groups = [[z_size * i + j for i in range(x_size)] for j in range(z_size)]
        pair = [(i, i ^ 1) for i in range(n_t)]

        packed = pl.pallas_call(
            pack_kernel, out_shape=sds((own_blocks, 2, tok, side), BF), in_specs=[vm(), vm()], out_specs=vm(),
            compiler_params=params(), name="pack",
        )(tokens, out_grad)
        act = lax.all_gather(packed.reshape(own_blocks * 2 * tok, side), "tensor", axis=0, tiled=True)
        act = act.reshape(blocks, 2, tok, side)

        per = side // n_dp
        bins, dpre = pl.pallas_call(
            lambda *refs: bins_kernel(bin_scale, n_dp, *refs),
            out_shape=(sds((n_dp, 2 * slots * per, side), BF), sds((col_count + 1, tok, side), BF)),
            in_specs=[sm(), sm(), vm(), vm(), vm()], out_specs=(vm(), vm()),
            scratch_shapes=[
                pltpu.VMEM((col_count + 1, tok, side), F32), pltpu.VMEM((col_count + 1, tok, side), F32),
                pltpu.VMEM((col_count + 1, tok, side), BF), pltpu.VMEM((n_dp, 2 * slots * per, side), F32),
            ],
            compiler_params=params(), cost_estimate=cost(4 * 2 * slots * tok * side * side, 8 * 2**20), name="bins",
        )(block_rows, block_cols, act, w_in, w_out)

        bins = bins.reshape(n_dp * 2 * slots * per, side)
        stage = lax.psum_scatter(bins, "dp", scatter_dimension=0, axis_index_groups=x_groups, tiled=True)

        keep, send = pl.pallas_call(
            back_kernel, out_shape=(sds((half, blocks * side), BF), sds((half, blocks * side), BF)),
            in_specs=[sm(), sm(), vm(), vm()], out_specs=(vm(), vm()),
            scratch_shapes=[pltpu.VMEM((blocks, tok, side), F32)],
            compiler_params=params(), cost_estimate=cost(2 * slots * tok * side * side, 4 * 2**20), name="back",
        )(block_rows, block_cols, dpre, w_in)
        got = lax.ppermute(send, "tensor", pair)
        two = (keep.astype(F32) + got.astype(F32)).astype(BF)
        width = blocks * side
        parts = lax.all_to_all(two.reshape(ny, half // ny, width), "tensor", 0, 0, axis_index_groups=y_groups, tiled=True)
        parts, stage = lax.optimization_barrier((parts, stage))
        sums = lax.psum_scatter(stage, "dp", scatter_dimension=0, axis_index_groups=z_groups, tiled=True)
        chunk = 1024
        spread = pl.pallas_call(
            spread_kernel, grid=(width // chunk,), out_shape=sds((ny, half // ny, width), BF),
            in_specs=[pl.BlockSpec((ny, half // ny, chunk), lambda i: (0, 0, i))],
            out_specs=pl.BlockSpec((ny, half // ny, chunk), lambda i: (0, 0, i)),
            compiler_params=params(), cost_estimate=cost(2**20, 2 * 2**20), name="spread",
        )(parts)
        mine = lax.all_to_all(spread, "tensor", 0, 0, axis_index_groups=y_groups, tiled=True).reshape(half, width)
        other = lax.ppermute(mine, "tensor", pair)
        in_grad = pl.pallas_call(
            join_kernel, out_shape=sds((tok, width), BF), in_specs=[hbm(), hbm()], out_specs=hbm(),
            scratch_shapes=[pltpu.SemaphoreType.DMA((2,))], compiler_params=params(),
            cost_estimate=cost(0, 4 * 2**20), name="join",
        )(mine, other)
        win_grad, wout_grad = pl.pallas_call(
            lambda *refs: finish_kernel(bin_scale, *refs),
            out_shape=(sds((slots, per * side), F32), sds((slots, per * side), F32)),
            in_specs=[vm()], out_specs=(vm(), vm()),
            scratch_shapes=[pltpu.VMEM((2 * slots * per, side), F32)], compiler_params=params(), name="finish",
        )(sums)
        return in_grad, win_grad, wout_grad

    return local


def solution(mesh):
    z_size = 8
    in_specs = (
        P("dp", "tensor"),
        P("dp", "tensor"),
        P("tensor", None, None),
        P("tensor", None, None),
        P("tensor", None),
        P("tensor", None),
    )
    out_specs = (P("dp", None), P("tensor", "dp"), P("tensor", "dp"))
    return jax.shard_map(make_local(z_size), mesh=mesh, in_specs=in_specs, out_specs=out_specs, check_vma=False)
```

```python
import jax
import jax.numpy as jnp
from jax import lax
from jax.experimental import pallas as pl
from jax.experimental.pallas import tpu as pltpu
from jax.sharding import PartitionSpec as P

FF = 14336
CLIP = 4.0
LANES = 128
BF = jnp.bfloat16
F32 = jnp.float32
VMEM_LIMIT = 40 * 1024 * 1024
VMEM_BINS = 61 * 1024 * 1024
VMEM_FULL = 63 * 1024 * 1024


def dot(a, b, ca, cb):
    return lax.dot_general(a, b, (((ca,), (cb,)), ((), ())), preferred_element_type=F32)


def slot_index(rows_ref, cols_ref, s, dead_col):
    row = rows_ref[0, s]
    live = row >= 0
    return jnp.where(live, row, 0), jnp.where(live, cols_ref[0, s], dead_col)


def pack_kernel(tok_ref, grad_ref, out_ref, sems):
    copies = []
    for b in range(out_ref.shape[0]):
        for k, ref in enumerate((tok_ref, grad_ref)):
            copies.append(pltpu.make_async_copy(ref.at[:, b * LANES : (b + 1) * LANES], out_ref.at[b, k], sems.at[2 * b + k]))
    for c in copies:
        c.start()
    for c in copies:
        c.wait()


def start_gather(rows_hbm, cols_hbm, act_ref, buf_ref, rows_ref, cols_ref, sems, isems, dead_col):
    icopies = [pltpu.make_async_copy(rows_hbm, rows_ref, isems.at[0]), pltpu.make_async_copy(cols_hbm, cols_ref, isems.at[1])]
    for c in icopies:
        c.start()
    for c in icopies:
        c.wait()
    index = [slot_index(rows_ref, cols_ref, s, dead_col) for s in range(buf_ref.shape[0])]
    copies = [pltpu.make_async_copy(act_ref.at[r], buf_ref.at[s], sems.at[s]) for s, (r, _) in enumerate(index)]
    for c in copies:
        c.start()
    return index, copies


def front_kernel(rows_hbm, cols_hbm, act_ref, win_hbm, wout_hbm, keep_ref, send_ref, dpre_ref, hid_ref,
                 buf_ref, win_ref, wout_ref, pre_ref, dh_ref, acc_ref, rows_ref, cols_ref, sems, isems, wsems):
    slots = win_ref.shape[0]
    col_count = pre_ref.shape[0] - 1
    wcopies = [pltpu.make_async_copy(win_hbm, win_ref, wsems.at[0]), pltpu.make_async_copy(wout_hbm, wout_ref, wsems.at[1])]
    for c in wcopies:
        c.start()
    index, copies = start_gather(rows_hbm, cols_hbm, act_ref, buf_ref, rows_ref, cols_ref, sems, isems, col_count)
    pre_ref[...] = jnp.zeros_like(pre_ref)
    dh_ref[...] = jnp.zeros_like(dh_ref)
    acc_ref[...] = jnp.zeros_like(acc_ref)
    hid_ref[col_count] = jnp.zeros(hid_ref.shape[1:], BF)
    dpre_ref[col_count] = jnp.zeros(dpre_ref.shape[1:], BF)
    for c in wcopies:
        c.wait()
    for s in range(slots):
        c = index[s][1]
        copies[s].wait()
        pre_ref[c] += dot(buf_ref[s, 0], win_ref[s], 1, 0)
        dh_ref[c] += dot(buf_ref[s, 1], wout_ref[s], 1, 1)
    for c in range(col_count):
        pre = pre_ref[c]
        sigma = jax.nn.sigmoid(pre)
        hid_ref[c] = (pre * sigma).astype(BF)
        dpre_ref[c] = (dh_ref[c] * sigma * (1.0 + pre * (1.0 - sigma))).astype(BF)
    for s in range(slots):
        r, c = index[s]
        acc_ref[r] += dot(dpre_ref[c], win_ref[s], 1, 1)
    ny = keep_ref.shape[0]
    half = acc_ref.shape[1] // 2
    rows = half // ny
    core = lax.rem(lax.axis_index("tensor"), 2)
    for out_ref, first in ((keep_ref, core * half), (send_ref, (1 - core) * half)):
        first = pl.multiple_of(first, half)
        for b in range(acc_ref.shape[0]):
            val = acc_ref[b, pl.ds(first, half), :].astype(BF)
            for y in range(ny):
                out_ref[y, b * rows : (b + 1) * rows, :] = val[y * rows : (y + 1) * rows]


def bins_kernel(bin_scale, order, rows_hbm, cols_hbm, act_ref, dpre_ref, hid_ref, bins_ref,
                buf_ref, wide_ref, rows_ref, cols_ref, sems, isems):
    slots = buf_ref.shape[0]
    groups = len(order)
    per = LANES // groups
    index, copies = start_gather(
        rows_hbm, cols_hbm, act_ref, buf_ref, rows_ref, cols_ref, sems, isems, dpre_ref.shape[0] - 1
    )

    def put(val, slot):
        val = jnp.floor(jnp.clip(val, -CLIP, CLIP) * bin_scale)
        for g in range(groups):
            wide_ref[order[g], slot * per : (slot + 1) * per, :] = val[g * per : (g + 1) * per]

    for s in range(slots):
        c = index[s][1]
        copies[s].wait()
        put(dot(buf_ref[s, 0], dpre_ref[c], 0, 0), s)
        put(dot(hid_ref[c], buf_ref[s, 1], 0, 0), slots + s)
    for g in range(groups):
        bins_ref[g] = wide_ref[g].astype(BF)


def spread_kernel(in_ref, out_ref):
    total = in_ref[0].astype(F32)
    for k in range(1, in_ref.shape[0]):
        total += in_ref[k].astype(F32)
    total = total.astype(BF)
    for k in range(out_ref.shape[0]):
        out_ref[k] = total


def join_kernel(mine_ref, other_ref, out_ref, wide_ref, sems):
    ny, high, _ = mine_ref.shape
    blocks = wide_ref.shape[1] // LANES
    rows = high // blocks
    half = ny * rows
    core = lax.rem(lax.axis_index("tensor"), 2)
    copies = []
    for k, (ref, base) in enumerate(((mine_ref, core * half), (other_ref, (1 - core) * half))):
        for y in range(ny):
            at = pl.ds(pl.multiple_of(base + y * rows, rows), rows)
            for b in range(blocks):
                wide_ref[at, b * LANES : (b + 1) * LANES] = ref[y, b * rows : (b + 1) * rows, :]
            copies.append(pltpu.make_async_copy(wide_ref.at[at], out_ref.at[at], sems.at[k * ny + y]))
            copies[-1].start()
    for c in copies:
        c.wait()


def finish_kernel(bin_scale, in_ref, win_ref, wout_ref, wide_ref):
    slots = win_ref.shape[0]
    per = in_ref.shape[1] // (2 * slots)
    total = in_ref[0].astype(F32)
    for k in range(1, in_ref.shape[0]):
        total += in_ref[k].astype(F32)
    wide_ref[...] = total / bin_scale
    for j in range(per):
        at = slice(j * LANES, (j + 1) * LANES)
        win_ref[:, at] = wide_ref[pl.ds(j, slots, stride=per), :]
        wout_ref[:, at] = wide_ref[pl.ds(slots * per + j, slots, stride=per), :]


def vm():
    return pl.BlockSpec(memory_space=pltpu.VMEM)


def hbm():
    return pl.BlockSpec(memory_space=pltpu.HBM)


def sds(shape, dtype):
    return jax.ShapeDtypeStruct(shape, dtype)


def params(limit=VMEM_LIMIT):
    return pltpu.CompilerParams(vmem_limit_bytes=limit)


def cost(flops, nbytes):
    return pl.CostEstimate(flops=flops, bytes_accessed=nbytes, transcendentals=0)


def dma(n):
    return pltpu.SemaphoreType.DMA((n,))


def make_local(z_size):
    def local(tokens, out_grad, w_in, w_out, block_rows, block_cols):
        n_dp = lax.axis_size("dp")
        n_t = lax.axis_size("tensor")
        bin_scale = 4194304.0 / n_dp
        tok, feat = tokens.shape
        slots, side, _ = w_in.shape
        own_blocks = feat // side
        blocks = own_blocks * n_t
        width = blocks * side
        cols = FF // side // n_t + 1
        ny = n_t // 2
        x_size = n_dp // z_size
        rows = tok // n_t
        per = side // n_dp
        y_groups = [[2 * i + c for i in range(ny)] for c in range(2)]
        z_groups = [[z_size * i + j for j in range(z_size)] for i in range(x_size)]
        x_groups = [[z_size * i + j for i in range(x_size)] for j in range(z_size)]
        pair = [(i, i ^ 1) for i in range(n_t)]
        order = [(p % z_size) * x_size + p // z_size for p in range(n_dp)]

        packed = pl.pallas_call(
            pack_kernel, out_shape=sds((own_blocks, 2, tok, side), BF), in_specs=[hbm(), hbm()], out_specs=hbm(),
            scratch_shapes=[dma(2 * own_blocks)], compiler_params=params(VMEM_FULL), name="pack",
        )(tokens, out_grad)
        act = lax.all_gather(packed.reshape(own_blocks * 2 * tok, side), "tensor", axis=0, tiled=True)
        act = act.reshape(blocks, 2, tok, side)

        piece = sds((ny, blocks * rows, side), BF)
        column = sds((cols, tok, side), BF)
        bins_shape = (n_dp, 2 * slots * per, side)
        index_scratch = [
            pltpu.SMEM(block_rows.shape, jnp.int32), pltpu.SMEM(block_cols.shape, jnp.int32), dma(slots), dma(2),
        ]
        keep, send, dpre, hid = pl.pallas_call(
            front_kernel, out_shape=(piece, piece, column, column), in_specs=[hbm()] * 5, out_specs=(vm(),) * 4,
            scratch_shapes=[
                pltpu.VMEM((slots, 2, tok, side), BF), pltpu.VMEM(w_in.shape, BF), pltpu.VMEM(w_out.shape, BF),
                pltpu.VMEM(column.shape, F32), pltpu.VMEM(column.shape, F32), pltpu.VMEM((blocks, tok, side), F32),
                *index_scratch, dma(2),
            ],
            compiler_params=params(VMEM_FULL), cost_estimate=cost(6 * slots * tok * side * side, 8 * 2**20), name="front",
        )(block_rows, block_cols, act, w_in, w_out)
        got = lax.ppermute(send, "tensor", pair)
        bins = pl.pallas_call(
            lambda *refs: bins_kernel(bin_scale, order, *refs),
            out_shape=sds(bins_shape, BF), in_specs=[hbm(), hbm(), hbm(), vm(), vm()], out_specs=vm(),
            scratch_shapes=[pltpu.VMEM((slots, 2, tok, side), BF), pltpu.VMEM(bins_shape, F32), *index_scratch],
            compiler_params=params(VMEM_BINS), cost_estimate=cost(4 * slots * tok * side * side, 6 * 2**20), name="bins",
        )(block_rows, block_cols, act, dpre, hid)
        stage = lax.psum_scatter(
            bins.reshape(n_dp * 2 * slots * per, side), "dp", scatter_dimension=0, axis_index_groups=z_groups, tiled=True
        )
        two = (keep.astype(F32) + got.astype(F32)).astype(BF)
        parts = lax.all_to_all(two, "tensor", 0, 0, axis_index_groups=y_groups, tiled=True)
        chunk = blocks * rows // 4
        spread = pl.pallas_call(
            spread_kernel, grid=(4,), out_shape=piece,
            in_specs=[pl.BlockSpec((ny, chunk, side), lambda i: (0, i, 0))],
            out_specs=pl.BlockSpec((ny, chunk, side), lambda i: (0, i, 0)),
            compiler_params=params(), cost_estimate=cost(2**20, 2 * 2**20), name="spread",
        )(parts)
        mine = lax.all_to_all(spread, "tensor", 0, 0, axis_index_groups=y_groups, tiled=True)
        other = lax.ppermute(mine, "tensor", pair)
        sums = lax.all_to_all(
            stage.reshape(x_size, 2 * slots * per, side), "dp", 0, 0, axis_index_groups=x_groups, tiled=True
        )
        in_grad = pl.pallas_call(
            join_kernel, out_shape=sds((tok, width), BF), in_specs=[vm(), vm()], out_specs=hbm(),
            scratch_shapes=[pltpu.VMEM((tok, width), BF), dma(2 * ny)], compiler_params=params(),
            cost_estimate=cost(0, 4 * 2**20), name="join",
        )(mine, other)
        win_grad, wout_grad = pl.pallas_call(
            lambda *refs: finish_kernel(bin_scale, *refs),
            out_shape=(sds((slots, per * side), F32), sds((slots, per * side), F32)),
            in_specs=[vm()], out_specs=(vm(), vm()),
            scratch_shapes=[pltpu.VMEM((2 * slots * per, side), F32)], compiler_params=params(), name="finish",
        )(sums)
        return in_grad, win_grad, wout_grad

    return local


def solution(mesh):
    z_size = 8
    in_specs = (
        P("dp", "tensor"),
        P("dp", "tensor"),
        P("tensor", None, None),
        P("tensor", None, None),
        P("tensor", None),
        P("tensor", None),
    )
    out_specs = (P("dp", None), P("tensor", "dp"), P("tensor", "dp"))
    return jax.shard_map(make_local(z_size), mesh=mesh, in_specs=in_specs, out_specs=out_specs, check_vma=False)
```

```python
import jax
import jax.numpy as jnp
from jax import lax
from jax.experimental import pallas as pl
from jax.experimental.pallas import tpu as pltpu
from jax.sharding import PartitionSpec as P

FF = 14336
CLIP = 4.0
LANES = 128
BF = jnp.bfloat16
F32 = jnp.float32
VMEM_LIMIT = 40 * 1024 * 1024
VMEM_FRONT = 62 * 1024 * 1024
VMEM_BACK = 60 * 1024 * 1024
VMEM_BINS = 61 * 1024 * 1024
VMEM_FULL = 63 * 1024 * 1024
PARTS = 8


def dot(a, b, ca, cb):
    return lax.dot_general(a, b, (((ca,), (cb,)), ((), ())), preferred_element_type=F32)


def slot_index(rows_ref, cols_ref, s, dead_col):
    row = rows_ref[0, s]
    live = row >= 0
    return jnp.where(live, row, 0), jnp.where(live, cols_ref[0, s], dead_col)


def pack_kernel(ny, tok_ref, grad_ref, out_ref):
    tok = tok_ref.shape[0]
    rows = tok // (2 * ny)
    for k, ref in enumerate((tok_ref, grad_ref)):
        for h in range(2):
            for y in range(ny):
                val = ref[(2 * y + h) * rows : (2 * y + h + 1) * rows, :]
                for b in range(out_ref.shape[0]):
                    out_ref[b, k, h, y * rows : (y + 1) * rows, :] = val[:, b * LANES : (b + 1) * LANES]


def load_index(index_hbm, index_ref, sem):
    return [pltpu.make_async_copy(h, r, sem.at[k]) for k, (h, r) in enumerate(zip(index_hbm, index_ref))]


def run_all(copies):
    for c in copies:
        c.start()


def wait_all(copies):
    for c in copies:
        c.wait()


def own_core():
    return lax.rem(lax.axis_index("tensor"), 2)


def front_kernel(rows_hbm, cols_hbm, rows2_hbm, cols2_hbm, act_hbm, win_hbm, wout_hbm, win2_hbm, wout2_hbm,
                 out_ref, mine_ref, theirs_ref, act_ref, win_ref, wout_ref, pre_ref, dh_ref, acc_ref,
                 rows_ref, cols_ref, rows2_ref, cols2_ref, isems, sems, wsems):
    slots = win_ref.shape[1]
    col_count = pre_ref.shape[1] - 1
    index_copies = load_index(
        (rows_hbm, cols_hbm, rows2_hbm, cols2_hbm), (rows_ref, cols_ref, rows2_ref, cols2_ref), isems
    )
    run_all(index_copies)
    core = own_core()
    step = act_ref.shape[0] // PARTS
    copies = [pltpu.make_async_copy(act_hbm.at[pl.ds(k * step, step), :, core], act_ref.at[pl.ds(k * step, step)], sems.at[k])
              for k in range(PARTS)]
    weights = ((win_hbm, win_ref, 0), (wout_hbm, wout_ref, 0), (win2_hbm, win_ref, 1), (wout2_hbm, wout_ref, 1))
    copies += [pltpu.make_async_copy(h, r.at[k], wsems.at[n]) for n, (h, r, k) in enumerate(weights)]
    run_all(copies)
    pre_ref[...] = jnp.zeros_like(pre_ref)
    dh_ref[...] = jnp.zeros_like(dh_ref)
    acc_ref[...] = jnp.zeros_like(acc_ref)
    outs = (mine_ref, theirs_ref)
    for ref in outs:
        for k in range(2):
            ref[k, col_count] = jnp.zeros(ref.shape[2:], BF)
    wait_all(index_copies)
    index = [[slot_index(a, b, s, col_count) for s in range(slots)]
             for a, b in ((rows_ref, cols_ref), (rows2_ref, cols2_ref))]
    wait_all(copies)
    for s in range(slots):
        for k in range(2):
            r, c = index[k][s]
            pre_ref[k, c] += dot(act_ref[r, 0], win_ref[k, s], 1, 0)
            dh_ref[k, c] += dot(act_ref[r, 1], wout_ref[k, s], 1, 1)
    for k in range(2):
        for c in range(col_count):
            pre = pre_ref[k, c]
            sigma = jax.nn.sigmoid(pre)
            outs[k][0, c] = (dh_ref[k, c] * sigma * (1.0 + pre * (1.0 - sigma))).astype(BF)
            outs[k][1, c] = (pre * sigma).astype(BF)
    for s in range(slots):
        for k in range(2):
            r, c = index[k][s]
            acc_ref[r] += dot(outs[k][0, c], win_ref[k, s], 1, 1)
    ny = out_ref.shape[0]
    rows = acc_ref.shape[1] // ny
    for b in range(acc_ref.shape[0]):
        val = acc_ref[b].astype(BF)
        for y in range(ny):
            out_ref[y, b * rows : (b + 1) * rows, :] = val[y * rows : (y + 1) * rows]


def bins_kernel(bin_scale, z_size, rows_hbm, cols_hbm, act_hbm, mine_ref, got_ref, *refs):
    n = len(refs) - 7
    bins_refs = refs[:n]
    act_ref, wide_ref, full_ref, rows_ref, cols_ref, isems, sems = refs[n:]
    slots = rows_ref.shape[1]
    groups = wide_ref.shape[0]
    per = LANES // groups
    half = mine_ref.shape[2]
    col_count = mine_ref.shape[1] - 1
    index_copies = load_index((rows_hbm, cols_hbm), (rows_ref, cols_ref), isems)
    step = act_ref.shape[0] // PARTS
    copies = [pltpu.make_async_copy(act_hbm.at[pl.ds(k * step, step)], act_ref.at[pl.ds(k * step, step)], sems.at[k])
              for k in range(PARTS)]
    run_all(index_copies)
    run_all(copies)
    core = own_core()
    for ref, first in ((mine_ref, core), (got_ref, 1 - core)):
        at = pl.ds(pl.multiple_of(first * half, half), half)
        for k in range(2):
            for c in range(col_count + 1):
                full_ref[k, c, at, :] = ref[k, c]
    wait_all(index_copies)
    index = [slot_index(rows_ref, cols_ref, s, col_count) for s in range(slots)]
    wait_all(copies)

    def put(val, slot):
        val = jnp.floor(jnp.clip(val, -CLIP, CLIP) * bin_scale)
        for g in range(groups):
            wide_ref[g, slot * per : (slot + 1) * per, :] = val[g * per : (g + 1) * per]

    for s in range(slots):
        r, c = index[s]
        put(dot(act_ref[r, 0].reshape(2 * half, LANES), full_ref[0, c], 0, 0), s)
        put(dot(full_ref[1, c], act_ref[r, 1].reshape(2 * half, LANES), 0, 0), slots + s)
    here = lax.axis_index("dp") // z_size
    for d in range(n):
        to = lax.rem(here + d, n)
        for z in range(z_size):
            bins_refs[d][z] = wide_ref[to * z_size + z].astype(BF)


def total_of(ref):
    total = ref[0].astype(F32)
    for k in range(1, ref.shape[0]):
        total += ref[k].astype(F32)
    return total


def rows_kernel(in_ref, out_ref):
    total = total_of(in_ref).astype(BF)
    rows, width = out_ref.shape
    for b in range(width // LANES):
        out_ref[:, b * LANES : (b + 1) * LANES] = total[b * rows : (b + 1) * rows]


def stage_kernel(*refs):
    total = refs[0][...].astype(F32)
    for ref in refs[1:-1]:
        total += ref[...].astype(F32)
    refs[-1][...] = total.astype(BF)


def finish_kernel(bin_scale, in_ref, win_ref, wout_ref, wide_ref):
    slots = win_ref.shape[0]
    per = in_ref.shape[1] // (2 * slots)
    wide_ref[...] = total_of(in_ref) / bin_scale
    for j in range(per):
        at = slice(j * LANES, (j + 1) * LANES)
        win_ref[:, at] = wide_ref[pl.ds(j, slots, stride=per), :]
        wout_ref[:, at] = wide_ref[pl.ds(slots * per + j, slots, stride=per), :]


def vm():
    return pl.BlockSpec(memory_space=pltpu.VMEM)


def hbm():
    return pl.BlockSpec(memory_space=pltpu.HBM)


def sds(shape, dtype):
    return jax.ShapeDtypeStruct(shape, dtype)


def params(limit=VMEM_LIMIT):
    return pltpu.CompilerParams(vmem_limit_bytes=limit)


def cost(flops, nbytes):
    return pl.CostEstimate(flops=flops, bytes_accessed=nbytes, transcendentals=0)


def dma(n):
    return pltpu.SemaphoreType.DMA((n,))


def make_local(z_size):
    def local(tokens, out_grad, w_in, w_out, block_rows, block_cols):
        n_dp = lax.axis_size("dp")
        n_t = lax.axis_size("tensor")
        bin_scale = 4194304.0 / n_dp
        tok, feat = tokens.shape
        slots, side, _ = w_in.shape
        own_blocks = feat // side
        blocks = own_blocks * n_t
        width = blocks * side
        cols = FF // side // n_t + 1
        ny = n_t // 2
        x_size = n_dp // z_size
        rows = tok // n_t
        per = side // n_dp
        y_groups = [[2 * i + c for i in range(ny)] for c in range(2)]
        z_groups = [[z_size * i + j for j in range(z_size)] for i in range(x_size)]
        pair = [(i, i ^ 1) for i in range(n_t)]

        half = tok // 2
        packed = pl.pallas_call(
            lambda *refs: pack_kernel(ny, *refs), out_shape=sds((own_blocks, 2, 2, half, side), BF),
            in_specs=[vm(), vm()], out_specs=vm(), compiler_params=params(VMEM_FULL), name="pack",
        )(tokens, out_grad)
        act = lax.all_gather(packed.reshape(own_blocks * 2 * tok, side), "tensor", axis=0, tiled=True)
        act = act.reshape(blocks, 2, 2, half, side)
        swapped = [lax.ppermute(v, "tensor", pair) for v in (block_rows, block_cols, w_in, w_out)]
        act, *swapped = lax.optimization_barrier((act, *swapped))
        rows2, cols2, w_in2, w_out2 = swapped

        columns = sds((2, cols, half, side), BF)
        piece = sds((ny, blocks * rows, side), BF)
        index_scratch = [pltpu.SMEM(block_rows.shape, jnp.int32), pltpu.SMEM(block_cols.shape, jnp.int32)]
        part, kept, sent = pl.pallas_call(
            front_kernel, out_shape=(piece, columns, columns), in_specs=[hbm()] * 9, out_specs=(vm(),) * 3,
            scratch_shapes=[
                pltpu.VMEM((blocks, 2, half, side), BF), pltpu.VMEM((2, *w_in.shape), BF), pltpu.VMEM((2, *w_out.shape), BF),
                pltpu.VMEM(columns.shape, F32), pltpu.VMEM(columns.shape, F32), pltpu.VMEM((blocks, half, side), F32),
                *index_scratch, *index_scratch, dma(4), dma(PARTS), dma(4),
            ],
            compiler_params=params(VMEM_FULL), cost_estimate=cost(6 * slots * tok * side * side, 10 * 2**20), name="front",
        )(block_rows, block_cols, rows2, cols2, act, w_in, w_out, w_in2, w_out2)
        parts = lax.all_to_all(part, "tensor", 0, 0, axis_index_groups=y_groups, tiled=True)

        got = lax.ppermute(sent, "tensor", pair)
        bins_shape = (n_dp, 2 * slots * per, side)
        pieces = pl.pallas_call(
            lambda *refs: bins_kernel(bin_scale, z_size, *refs),
            out_shape=(sds((z_size, 2 * slots * per, side), BF),) * x_size,
            in_specs=[hbm(), hbm(), hbm(), vm(), vm()], out_specs=(vm(),) * x_size,
            scratch_shapes=[
                pltpu.VMEM(act.shape, BF), pltpu.VMEM(bins_shape, F32), pltpu.VMEM((2, cols, tok, side), BF),
                *index_scratch, dma(2), dma(PARTS),
            ],
            compiler_params=params(VMEM_BINS), cost_estimate=cost(4 * slots * tok * side * side, 6 * 2**20), name="bins",
        )(block_rows, block_cols, act, kept, got)
        by_x = [pieces[0]]
        for d in range(1, x_size):
            by_x.append(lax.ppermute(pieces[d], "dp", [(p, (p + d * z_size) % n_dp) for p in range(n_dp)]))

        own = pl.pallas_call(
            rows_kernel, out_shape=sds((rows, width), BF), in_specs=[vm()], out_specs=vm(), compiler_params=params(),
            cost_estimate=cost(2**20, 2 * 2**20), name="rows",
        )(parts)
        own, by_x[0] = lax.optimization_barrier((own, by_x[0]))
        in_grad = lax.all_gather(own, "tensor", axis=0, tiled=True)

        stage = pl.pallas_call(
            stage_kernel, grid=(4,), out_shape=sds(by_x[0].shape, BF),
            in_specs=[pl.BlockSpec((z_size // 4, 2 * slots * per, side), lambda i: (i, 0, 0))] * x_size,
            out_specs=pl.BlockSpec((z_size // 4, 2 * slots * per, side), lambda i: (i, 0, 0)),
            compiler_params=params(), cost_estimate=cost(2**20, 2 * 2**20), name="stage",
        )(*by_x)
        sums = lax.all_to_all(stage, "dp", 0, 0, axis_index_groups=z_groups, tiled=True)
        win_grad, wout_grad = pl.pallas_call(
            lambda *refs: finish_kernel(bin_scale, *refs),
            out_shape=(sds((slots, per * side), F32), sds((slots, per * side), F32)),
            in_specs=[vm()], out_specs=(vm(), vm()),
            scratch_shapes=[pltpu.VMEM((2 * slots * per, side), F32)], compiler_params=params(), name="finish",
        )(sums)
        return in_grad, win_grad, wout_grad

    return local


def solution(mesh):
    z_size = 8
    in_specs = (
        P("dp", "tensor"),
        P("dp", "tensor"),
        P("tensor", None, None),
        P("tensor", None, None),
        P("tensor", None),
        P("tensor", None),
    )
    out_specs = (P("dp", None), P("tensor", "dp"), P("tensor", "dp"))
    return jax.shard_map(make_local(z_size), mesh=mesh, in_specs=in_specs, out_specs=out_specs, check_vma=False)
```

```python
import jax
import jax.numpy as jnp
from jax import lax
from jax.experimental import pallas as pl
from jax.experimental.pallas import tpu as pltpu
from jax.sharding import PartitionSpec as P

FF = 14336
CLIP = 4.0
LANES = 128
BF = jnp.bfloat16
F32 = jnp.float32
VMEM_LIMIT = 40 * 1024 * 1024
VMEM_FRONT = 62 * 1024 * 1024
VMEM_BACK = 60 * 1024 * 1024
VMEM_BINS = 61 * 1024 * 1024
VMEM_FULL = 63 * 1024 * 1024
PARTS = 8


def dot(a, b, ca, cb):
    return lax.dot_general(a, b, (((ca,), (cb,)), ((), ())), preferred_element_type=F32)


def slot_index(rows_ref, cols_ref, s, dead_col):
    row = rows_ref[0, s]
    live = row >= 0
    return jnp.where(live, row, 0), jnp.where(live, cols_ref[0, s], dead_col)


def pack_kernel(ny, tok_ref, grad_ref, out_ref):
    tok = tok_ref.shape[0]
    rows = tok // (2 * ny)
    for k, ref in enumerate((tok_ref, grad_ref)):
        for h in range(2):
            for y in range(ny):
                val = ref[(2 * y + h) * rows : (2 * y + h + 1) * rows, :]
                for b in range(out_ref.shape[0]):
                    out_ref[b, k, h, y * rows : (y + 1) * rows, :] = val[:, b * LANES : (b + 1) * LANES]


def load_index(index_hbm, index_ref, sem):
    return [pltpu.make_async_copy(h, r, sem.at[k]) for k, (h, r) in enumerate(zip(index_hbm, index_ref))]


def run_all(copies):
    for c in copies:
        c.start()


def wait_all(copies):
    for c in copies:
        c.wait()


def own_core():
    return lax.rem(lax.axis_index("tensor"), 2)


def front_kernel(rows_hbm, cols_hbm, rows2_hbm, cols2_hbm, act_hbm, win_hbm, wout_hbm, win2_hbm, wout2_hbm,
                 out_ref, mine_ref, theirs_ref, act_ref, win_ref, wout_ref, pre_ref, dh_ref, acc_ref,
                 rows_ref, cols_ref, rows2_ref, cols2_ref, isems, sems, wsems):
    slots = win_ref.shape[1]
    col_count = pre_ref.shape[1] - 1
    index_copies = load_index(
        (rows_hbm, cols_hbm, rows2_hbm, cols2_hbm), (rows_ref, cols_ref, rows2_ref, cols2_ref), isems
    )
    run_all(index_copies)
    core = own_core()
    step = act_ref.shape[0] // PARTS
    copies = [pltpu.make_async_copy(act_hbm.at[pl.ds(k * step, step), :, core], act_ref.at[pl.ds(k * step, step)], sems.at[k])
              for k in range(PARTS)]
    weights = ((win_hbm, win_ref, 0), (wout_hbm, wout_ref, 0), (win2_hbm, win_ref, 1), (wout2_hbm, wout_ref, 1))
    copies += [pltpu.make_async_copy(h, r.at[k], wsems.at[n]) for n, (h, r, k) in enumerate(weights)]
    run_all(copies)
    pre_ref[...] = jnp.zeros_like(pre_ref)
    dh_ref[...] = jnp.zeros_like(dh_ref)
    acc_ref[...] = jnp.zeros_like(acc_ref)
    outs = (mine_ref, theirs_ref)
    for ref in outs:
        for k in range(2):
            ref[k, col_count] = jnp.zeros(ref.shape[2:], BF)
    wait_all(index_copies)
    index = [[slot_index(a, b, s, col_count) for s in range(slots)]
             for a, b in ((rows_ref, cols_ref), (rows2_ref, cols2_ref))]
    wait_all(copies)
    for s in range(slots):
        for k in range(2):
            r, c = index[k][s]
            pre_ref[k, c] += dot(act_ref[r, 0], win_ref[k, s], 1, 0)
            dh_ref[k, c] += dot(act_ref[r, 1], wout_ref[k, s], 1, 1)
    for k in range(2):
        for c in range(col_count):
            pre = pre_ref[k, c]
            sigma = jax.nn.sigmoid(pre)
            outs[k][0, c] = (dh_ref[k, c] * sigma * (1.0 + pre * (1.0 - sigma))).astype(BF)
            outs[k][1, c] = (pre * sigma).astype(BF)
    for s in range(slots):
        for k in range(2):
            r, c = index[k][s]
            acc_ref[r] += dot(outs[k][0, c], win_ref[k, s], 1, 1)
    ny = out_ref.shape[0]
    rows = acc_ref.shape[1] // ny
    for b in range(acc_ref.shape[0]):
        val = acc_ref[b].astype(BF)
        for y in range(ny):
            out_ref[y, b * rows : (b + 1) * rows, :] = val[y * rows : (y + 1) * rows]


def bins_kernel(bin_scale, z_size, rows_hbm, cols_hbm, act_hbm, mine_ref, got_ref, *refs):
    n = len(refs) - 7
    bins_refs = refs[:n]
    act_ref, wide_ref, full_ref, rows_ref, cols_ref, isems, sems = refs[n:]
    slots = rows_ref.shape[1]
    groups = wide_ref.shape[0]
    per = LANES // groups
    half = mine_ref.shape[2]
    col_count = mine_ref.shape[1] - 1
    index_copies = load_index((rows_hbm, cols_hbm), (rows_ref, cols_ref), isems)
    step = act_ref.shape[0] // PARTS
    copies = [pltpu.make_async_copy(act_hbm.at[pl.ds(k * step, step)], act_ref.at[pl.ds(k * step, step)], sems.at[k])
              for k in range(PARTS)]
    run_all(index_copies)
    run_all(copies)
    core = own_core()
    for ref, first in ((mine_ref, core), (got_ref, 1 - core)):
        at = pl.ds(pl.multiple_of(first * half, half), half)
        for k in range(2):
            for c in range(col_count + 1):
                full_ref[k, c, at, :] = ref[k, c]
    wait_all(index_copies)
    index = [slot_index(rows_ref, cols_ref, s, col_count) for s in range(slots)]
    wait_all(copies)

    def put(val, slot):
        val = jnp.floor(jnp.clip(val, -CLIP, CLIP) * bin_scale)
        for g in range(groups):
            wide_ref[g, slot * per : (slot + 1) * per, :] = val[g * per : (g + 1) * per]

    for s in range(slots):
        r, c = index[s]
        put(dot(act_ref[r, 0].reshape(2 * half, LANES), full_ref[0, c], 0, 0), s)
        put(dot(full_ref[1, c], act_ref[r, 1].reshape(2 * half, LANES), 0, 0), slots + s)
    here = lax.axis_index("dp") // z_size
    for d in range(n):
        to = lax.rem(here + d, n)
        for z in range(z_size):
            bins_refs[d][z] = wide_ref[to * z_size + z].astype(BF)


def total_of(ref):
    total = ref[0].astype(F32)
    for k in range(1, ref.shape[0]):
        total += ref[k].astype(F32)
    return total


def rows_kernel(in_ref, out_ref):
    total = total_of(in_ref).astype(BF)
    rows, width = out_ref.shape
    for b in range(width // LANES):
        out_ref[:, b * LANES : (b + 1) * LANES] = total[b * rows : (b + 1) * rows]


def stage_kernel(*refs):
    total = refs[0][...].astype(F32)
    for ref in refs[1:-1]:
        total += ref[...].astype(F32)
    refs[-1][...] = total.astype(BF)


def place_kernel(in_ref, out_ref, buf_ref, in_sems, out_sems):
    parts = in_sems.shape[0]
    step = buf_ref.shape[0] // parts
    at = [pl.ds(k * step, step) for k in range(parts)]
    loads = [pltpu.make_async_copy(in_ref.at[at[k]], buf_ref.at[at[k]], in_sems.at[k]) for k in range(parts)]
    stores = [pltpu.make_async_copy(buf_ref.at[at[k]], out_ref.at[at[k]], out_sems.at[k]) for k in range(parts)]
    run_all(loads)
    for k in range(parts):
        loads[k].wait()
        stores[k].start()
    wait_all(stores)


def finish_kernel(bin_scale, in_ref, win_ref, wout_ref, wide_ref):
    slots = win_ref.shape[0]
    per = in_ref.shape[1] // (2 * slots)
    wide_ref[...] = total_of(in_ref) / bin_scale
    for j in range(per):
        at = slice(j * LANES, (j + 1) * LANES)
        win_ref[:, at] = wide_ref[pl.ds(j, slots, stride=per), :]
        wout_ref[:, at] = wide_ref[pl.ds(slots * per + j, slots, stride=per), :]


def vm():
    return pl.BlockSpec(memory_space=pltpu.VMEM)


def hbm():
    return pl.BlockSpec(memory_space=pltpu.HBM)


def sds(shape, dtype):
    return jax.ShapeDtypeStruct(shape, dtype)


def params(limit=VMEM_LIMIT):
    return pltpu.CompilerParams(vmem_limit_bytes=limit)


def cost(flops, nbytes):
    return pl.CostEstimate(flops=flops, bytes_accessed=nbytes, transcendentals=0)


def dma(n):
    return pltpu.SemaphoreType.DMA((n,))


def make_local(z_size):
    def local(tokens, out_grad, w_in, w_out, block_rows, block_cols):
        n_dp = lax.axis_size("dp")
        n_t = lax.axis_size("tensor")
        bin_scale = 4194304.0 / n_dp
        tok, feat = tokens.shape
        slots, side, _ = w_in.shape
        own_blocks = feat // side
        blocks = own_blocks * n_t
        width = blocks * side
        cols = FF // side // n_t + 1
        ny = n_t // 2
        x_size = n_dp // z_size
        rows = tok // n_t
        per = side // n_dp
        y_groups = [[2 * i + c for i in range(ny)] for c in range(2)]
        z_groups = [[z_size * i + j for j in range(z_size)] for i in range(x_size)]
        pair = [(i, i ^ 1) for i in range(n_t)]

        half = tok // 2
        packed = pl.pallas_call(
            lambda *refs: pack_kernel(ny, *refs), out_shape=sds((own_blocks, 2, 2, half, side), BF),
            in_specs=[vm(), vm()], out_specs=vm(), compiler_params=params(VMEM_FULL), name="pack",
        )(tokens, out_grad)
        act = lax.all_gather(packed.reshape(own_blocks * 2 * tok, side), "tensor", axis=0, tiled=True)
        act = act.reshape(blocks, 2, 2, half, side)
        swapped = [lax.ppermute(v, "tensor", pair) for v in (block_rows, block_cols, w_in, w_out)]
        act, *swapped = lax.optimization_barrier((act, *swapped))
        rows2, cols2, w_in2, w_out2 = swapped

        columns = sds((2, cols, half, side), BF)
        piece = sds((ny, blocks * rows, side), BF)
        index_scratch = [pltpu.SMEM(block_rows.shape, jnp.int32), pltpu.SMEM(block_cols.shape, jnp.int32)]
        part, kept, sent = pl.pallas_call(
            front_kernel, out_shape=(piece, columns, columns), in_specs=[hbm()] * 9, out_specs=(vm(),) * 3,
            scratch_shapes=[
                pltpu.VMEM((blocks, 2, half, side), BF), pltpu.VMEM((2, *w_in.shape), BF), pltpu.VMEM((2, *w_out.shape), BF),
                pltpu.VMEM(columns.shape, F32), pltpu.VMEM(columns.shape, F32), pltpu.VMEM((blocks, half, side), F32),
                *index_scratch, *index_scratch, dma(4), dma(PARTS), dma(4),
            ],
            compiler_params=params(VMEM_FULL), cost_estimate=cost(6 * slots * tok * side * side, 10 * 2**20), name="front",
        )(block_rows, block_cols, rows2, cols2, act, w_in, w_out, w_in2, w_out2)
        parts = lax.all_to_all(part, "tensor", 0, 0, axis_index_groups=y_groups, tiled=True)

        got = lax.ppermute(sent, "tensor", pair)
        bins_shape = (n_dp, 2 * slots * per, side)
        pieces = pl.pallas_call(
            lambda *refs: bins_kernel(bin_scale, z_size, *refs),
            out_shape=(sds((z_size, 2 * slots * per, side), BF),) * x_size,
            in_specs=[hbm(), hbm(), hbm(), vm(), vm()], out_specs=(vm(),) * x_size,
            scratch_shapes=[
                pltpu.VMEM(act.shape, BF), pltpu.VMEM(bins_shape, F32), pltpu.VMEM((2, cols, tok, side), BF),
                *index_scratch, dma(2), dma(PARTS),
            ],
            compiler_params=params(VMEM_BINS), cost_estimate=cost(4 * slots * tok * side * side, 6 * 2**20), name="bins",
        )(block_rows, block_cols, act, kept, got)
        by_x = [pieces[0]]
        for d in range(1, x_size):
            by_x.append(lax.ppermute(pieces[d], "dp", [(p, (p + d * z_size) % n_dp) for p in range(n_dp)]))

        own = pl.pallas_call(
            rows_kernel, out_shape=sds((rows, width), BF), in_specs=[vm()], out_specs=vm(), compiler_params=params(),
            cost_estimate=cost(2**20, 2 * 2**20), name="rows",
        )(parts)
        near = [0, 1, x_size - 1]
        own, *tied = lax.optimization_barrier((own, *(by_x[d] for d in near)))
        for d, v in zip(near, tied):
            by_x[d] = v
        in_grad = lax.all_gather(own, "tensor", axis=0, tiled=True)
        in_grad = pl.pallas_call(
            place_kernel, out_shape=sds((tok, width), BF), in_specs=[hbm()], out_specs=hbm(),
            scratch_shapes=[pltpu.VMEM((tok, width), BF), dma(PARTS), dma(PARTS)],
            compiler_params=params(VMEM_FULL), cost_estimate=cost(0, 4 * 2**20), name="place",
        )(in_grad)

        stage = pl.pallas_call(
            stage_kernel, grid=(4,), out_shape=sds(by_x[0].shape, BF),
            in_specs=[pl.BlockSpec((z_size // 4, 2 * slots * per, side), lambda i: (i, 0, 0))] * x_size,
            out_specs=pl.BlockSpec((z_size // 4, 2 * slots * per, side), lambda i: (i, 0, 0)),
            compiler_params=params(), cost_estimate=cost(2**20, 2 * 2**20), name="stage",
        )(*by_x)
        sums = lax.all_to_all(stage, "dp", 0, 0, axis_index_groups=z_groups, tiled=True)
        win_grad, wout_grad = pl.pallas_call(
            lambda *refs: finish_kernel(bin_scale, *refs),
            out_shape=(sds((slots, per * side), F32), sds((slots, per * side), F32)),
            in_specs=[vm()], out_specs=(vm(), vm()),
            scratch_shapes=[pltpu.VMEM((2 * slots * per, side), F32)], compiler_params=params(), name="finish",
        )(sums)
        return in_grad, win_grad, wout_grad

    return local


def solution(mesh):
    z_size = 8
    in_specs = (
        P("dp", "tensor"),
        P("dp", "tensor"),
        P("tensor", None, None),
        P("tensor", None, None),
        P("tensor", None),
        P("tensor", None),
    )
    out_specs = (P("dp", None), P("tensor", "dp"), P("tensor", "dp"))
    return jax.shard_map(make_local(z_size), mesh=mesh, in_specs=in_specs, out_specs=out_specs, check_vma=False)
```

```python
import jax
import jax.numpy as jnp
from jax import lax
from jax.experimental import pallas as pl
from jax.experimental.pallas import tpu as pltpu
from jax.sharding import PartitionSpec as P

FF = 14336
CLIP = 4.0
LANES = 128
BF = jnp.bfloat16
F32 = jnp.float32
VMEM_LIMIT = 40 * 1024 * 1024
VMEM_FRONT = 57 * 1024 * 1024
VMEM_BACK = 60 * 1024 * 1024
VMEM_BINS = 61 * 1024 * 1024
VMEM_FULL = 63 * 1024 * 1024
PARTS = 8
CHUNKS = 2


def dot(a, b, ca, cb):
    return lax.dot_general(a, b, (((ca,), (cb,)), ((), ())), preferred_element_type=F32)


def slot_index(table_ref, s, dead_col):
    row = table_ref[0, s]
    live = row >= 0
    return jnp.where(live, row, 0), jnp.where(live, table_ref[1, s], dead_col)


def pack_kernel(ny, tok_ref, grad_ref, keep_ref, send_ref):
    tok = tok_ref.shape[0]
    rows = tok // (2 * ny)
    core = own_core()
    for k, ref in enumerate((tok_ref, grad_ref)):
        for out_ref, h in ((keep_ref, core), (send_ref, 1 - core)):
            for y in range(ny):
                val = ref[pl.ds(pl.multiple_of((2 * y + h) * rows, rows), rows), :]
                for b in range(out_ref.shape[0]):
                    out_ref[b, k, y * rows : (y + 1) * rows, :] = val[:, b * LANES : (b + 1) * LANES]


def load_index(index_hbm, index_ref, sem):
    return [pltpu.make_async_copy(h, r, sem.at[k]) for k, (h, r) in enumerate(zip(index_hbm, index_ref))]


def run_all(copies):
    for c in copies:
        c.start()


def wait_all(copies):
    for c in copies:
        c.wait()


def own_core():
    return lax.rem(lax.axis_index("tensor"), 2)


def front_kernel(ny, table_hbm, table2_hbm, win_hbm, wout_hbm, win2_hbm, wout2_hbm, *refs):
    ring, refs = refs[: ny + 1], refs[ny + 1 :]
    front_body(ny, table_hbm, table2_hbm, win_hbm, wout_hbm, win2_hbm, wout2_hbm, ring, *refs)


def ring_copies(ny, ring, act_ref, sems):
    core = own_core()
    y = lax.axis_index("tensor") // 2
    per = act_ref.shape[0] // ny
    half = per // 2
    copies = []

    def add(src, chip, part):
        first = (lax.rem(chip + ny, ny) * per) + (core if part == 0 else 1 - core) * half
        copies.append(pltpu.make_async_copy(src, act_ref.at[pl.ds(first, half)], sems.at[len(copies)]))

    reach = ny // 2
    shifts = [0] + [-d for d in range(1, reach)] + [d for d in range(1, reach)]
    for ref, d in zip(ring, shifts):
        for part in range(2):
            add(ref.at[pl.ds(part * half, half)], y + d, part)
    add(ring[-2], y - reach, 0)
    add(ring[-1], y + reach, 1)
    return copies


def front_body(ny, table_hbm, table2_hbm, win_hbm, wout_hbm, win2_hbm, wout2_hbm, ring,
               out_hbm, mine_hbm, theirs_hbm, act_hbm, act_ref, win_ref, wout_ref, pre_ref, dh_ref, acc_ref,
                 out_ref, mine_ref, theirs_ref, table_ref, table2_ref, isems, sems, wsems, osems):
    slots = win_ref.shape[1]
    col_count = pre_ref.shape[1] - 1
    run = slots // CHUNKS
    index_copies = load_index((table_hbm, table2_hbm), (table_ref, table2_ref), isems)
    run_all(index_copies)
    copies = ring_copies(ny, ring, act_ref, sems)
    weights = ((win_hbm, win_ref, 0), (wout_hbm, wout_ref, 0), (win2_hbm, win_ref, 1), (wout2_hbm, wout_ref, 1))
    chunks = [[pltpu.make_async_copy(h.at[pl.ds(n * run, run)], r.at[k, pl.ds(n * run, run)], wsems.at[4 * n + m])
               for m, (h, r, k) in enumerate(weights)] for n in range(CHUNKS)]
    run_all(copies)
    for c in chunks:
        run_all(c)
    pre_ref[...] = jnp.zeros_like(pre_ref)
    dh_ref[...] = jnp.zeros_like(dh_ref)
    acc_ref[...] = jnp.zeros_like(acc_ref)
    outs = (mine_ref, theirs_ref)
    for ref in outs:
        for k in range(2):
            ref[k, col_count] = jnp.zeros(ref.shape[2:], BF)
    wait_all(index_copies)
    index = [[slot_index(ref, s, col_count) for s in range(slots)] for ref in (table_ref, table2_ref)]
    wait_all(copies)
    leaving = [pltpu.make_async_copy(act_ref, act_hbm, osems.at[4])]
    run_all(leaving)
    for n in range(CHUNKS):
        wait_all(chunks[n])
        for k in range(2):
            for s in range(n * run, (n + 1) * run):
                r, c = index[k][s]
                pre_ref[k, c] += dot(act_ref[r, 0], win_ref[k, s], 1, 0)
                dh_ref[k, c] += dot(act_ref[r, 1], wout_ref[k, s], 1, 1)
    for k in (1, 0):
        for c in range(col_count):
            pre = pre_ref[k, c]
            sigma = jax.nn.sigmoid(pre)
            outs[k][0, c] = (dh_ref[k, c] * sigma * (1.0 + pre * (1.0 - sigma))).astype(BF)
            outs[k][1, c] = (pre * sigma).astype(BF)
    for n, (src, dst) in enumerate(((theirs_ref, theirs_hbm), (mine_ref, mine_hbm))):
        leaving.append(pltpu.make_async_copy(src, dst, osems.at[n]))
        leaving[-1].start()
    for k in range(2):
        for s in range(slots):
            r, c = index[k][s]
            acc_ref[r] += dot(outs[k][0, c], win_ref[k, s], 1, 1)
    rows = acc_ref.shape[1] // ny
    part = ny // 2
    for n in range(2):
        for b in range(acc_ref.shape[0]):
            val = acc_ref[b, n * part * rows : (n + 1) * part * rows, :].astype(BF)
            for y in range(part):
                out_ref[n * part + y, b * rows : (b + 1) * rows, :] = val[y * rows : (y + 1) * rows]
        at = pl.ds(n * part, part)
        leaving.append(pltpu.make_async_copy(out_ref.at[at], out_hbm.at[at], osems.at[2 + n]))
        leaving[-1].start()
    wait_all(leaving)


def bins_kernel(bin_scale, z_size, table_hbm, act_hbm, act2_hbm, mine_ref, got_ref, *refs):
    n = len(refs) - 6
    bins_refs = refs[:n]
    act_ref, wide_ref, full_ref, table_ref, isems, sems = refs[n:]
    slots = table_ref.shape[1]
    groups = wide_ref.shape[0]
    per = LANES // groups
    half = mine_ref.shape[2]
    col_count = mine_ref.shape[1] - 1
    index_copies = load_index((table_hbm,), (table_ref,), isems)
    core = own_core()
    copies = [pltpu.make_async_copy(act_hbm, act_ref.at[:, :, core], sems.at[0]),
              pltpu.make_async_copy(act2_hbm, act_ref.at[:, :, 1 - core], sems.at[1])]
    run_all(index_copies)
    run_all(copies)
    for ref, first in ((mine_ref, core), (got_ref, 1 - core)):
        at = pl.ds(pl.multiple_of(first * half, half), half)
        for k in range(2):
            for c in range(col_count + 1):
                full_ref[k, c, at, :] = ref[k, c]
    wait_all(index_copies)
    index = [slot_index(table_ref, s, col_count) for s in range(slots)]
    wait_all(copies)

    def put(val, slot):
        val = jnp.floor(jnp.clip(val, -CLIP, CLIP) * bin_scale)
        for g in range(groups):
            wide_ref[g, slot * per : (slot + 1) * per, :] = val[g * per : (g + 1) * per]

    for s in range(slots):
        r, c = index[s]
        put(dot(act_ref[r, 0].reshape(2 * half, LANES), full_ref[0, c], 0, 0), s)
        put(dot(full_ref[1, c], act_ref[r, 1].reshape(2 * half, LANES), 0, 0), slots + s)
    here = lax.axis_index("dp") // z_size
    for d in range(n):
        to = lax.rem(here + d, n)
        for z in range(z_size):
            bins_refs[d][z] = wide_ref[to * z_size + z].astype(BF)


def total_of(ref):
    total = ref[0].astype(F32)
    for k in range(1, ref.shape[0]):
        total += ref[k].astype(F32)
    return total


def rows_kernel(in_ref, out_ref):
    total = total_of(in_ref).astype(BF)
    rows, width = out_ref.shape
    for b in range(width // LANES):
        out_ref[:, b * LANES : (b + 1) * LANES] = total[b * rows : (b + 1) * rows]


def stage_kernel(*refs):
    total = refs[0][...].astype(F32)
    for ref in refs[1:-1]:
        total += ref[...].astype(F32)
    refs[-1][...] = total.astype(BF)


def place_kernel(in_ref, out_ref, buf_ref, in_sems, out_sems):
    parts = in_sems.shape[0]
    step = buf_ref.shape[0] // parts
    at = [pl.ds(k * step, step) for k in range(parts)]
    loads = [pltpu.make_async_copy(in_ref.at[at[k]], buf_ref.at[at[k]], in_sems.at[k]) for k in range(parts)]
    stores = [pltpu.make_async_copy(buf_ref.at[at[k]], out_ref.at[at[k]], out_sems.at[k]) for k in range(parts)]
    run_all(loads)
    for k in range(parts):
        loads[k].wait()
        stores[k].start()
    wait_all(stores)


def finish_kernel(bin_scale, in_ref, win_ref, wout_ref, wide_ref):
    slots = win_ref.shape[0]
    per = in_ref.shape[1] // (2 * slots)
    wide_ref[...] = total_of(in_ref) / bin_scale
    for j in range(per):
        at = slice(j * LANES, (j + 1) * LANES)
        win_ref[:, at] = wide_ref[pl.ds(j, slots, stride=per), :]
        wout_ref[:, at] = wide_ref[pl.ds(slots * per + j, slots, stride=per), :]


def vm():
    return pl.BlockSpec(memory_space=pltpu.VMEM)


def free():
    return pl.BlockSpec(memory_space=pl.ANY)


def hbm():
    return pl.BlockSpec(memory_space=pltpu.HBM)


def sds(shape, dtype):
    return jax.ShapeDtypeStruct(shape, dtype)


def params(limit=VMEM_LIMIT):
    return pltpu.CompilerParams(vmem_limit_bytes=limit)


def cost(flops, nbytes):
    return pl.CostEstimate(flops=flops, bytes_accessed=nbytes, transcendentals=0)


def dma(n):
    return pltpu.SemaphoreType.DMA((n,))


def make_local(z_size):
    def local(tokens, out_grad, w_in, w_out, block_rows, block_cols):
        n_dp = lax.axis_size("dp")
        n_t = lax.axis_size("tensor")
        bin_scale = 4194304.0 / n_dp
        tok, feat = tokens.shape
        slots, side, _ = w_in.shape
        own_blocks = feat // side
        blocks = own_blocks * n_t
        width = blocks * side
        cols = FF // side // n_t + 1
        ny = n_t // 2
        x_size = n_dp // z_size
        rows = tok // n_t
        per = side // n_dp
        y_groups = [[2 * i + c for i in range(ny)] for c in range(2)]
        z_groups = [[z_size * i + j for j in range(z_size)] for i in range(x_size)]
        pair = [(i, i ^ 1) for i in range(n_t)]

        half = tok // 2
        chunk = sds((own_blocks, 2, half, side), BF)
        keep, send = pl.pallas_call(
            lambda *refs: pack_kernel(ny, *refs), out_shape=(chunk, chunk),
            in_specs=[vm(), vm()], out_specs=(vm(), vm()), compiler_params=params(VMEM_FULL), name="pack",
        )(tokens, out_grad)
        other = lax.ppermute(send, "tensor", pair)
        chip = jnp.concatenate([keep, other])
        up = [(i, (i + 2) % n_t) for i in range(n_t)]
        down = [(i, (i - 2) % n_t) for i in range(n_t)]
        ups, downs = [chip], [chip]
        slot_table = jnp.concatenate([block_rows, block_cols])
        slot_table2 = lax.ppermute(slot_table, "tensor", pair)
        for d in range(1, ny // 2):
            if d == 2:
                ups[-1], slot_table2 = lax.optimization_barrier((ups[-1], slot_table2))
            ups.append(lax.ppermute(ups[-1], "tensor", up))
            downs.append(lax.ppermute(downs[-1], "tensor", down))
        ups.append(lax.ppermute(ups[-1][:own_blocks], "tensor", up))
        downs.append(lax.ppermute(downs[-1][own_blocks:], "tensor", down))
        ring = ups[:-1] + downs[1:-1] + [ups[-1], downs[-1]]
        w_in2, w_out2 = (lax.ppermute(v, "tensor", pair) for v in (w_in, w_out))

        columns = sds((2, cols, half, side), BF)
        piece = sds((ny, blocks * rows, side), BF)
        act_half = sds((blocks, 2, half, side), BF)
        index_scratch = [pltpu.SMEM(slot_table.shape, jnp.int32)]
        part, kept, sent, act = pl.pallas_call(
            lambda *refs: front_kernel(ny, *refs), out_shape=(piece, columns, columns, act_half),
            in_specs=[free()] * (6 + len(ring)), out_specs=(hbm(),) * 4,
            scratch_shapes=[
                pltpu.VMEM(act_half.shape, BF), pltpu.VMEM((2, *w_in.shape), BF), pltpu.VMEM((2, *w_out.shape), BF),
                pltpu.VMEM(columns.shape, F32), pltpu.VMEM(columns.shape, F32), pltpu.VMEM((blocks, half, side), F32),
                pltpu.VMEM(piece.shape, BF), pltpu.VMEM(columns.shape, BF), pltpu.VMEM(columns.shape, BF),
                *index_scratch, *index_scratch, dma(2), dma(2 * ny), dma(4 * CHUNKS), dma(5),
            ],
            compiler_params=params(VMEM_FRONT), cost_estimate=cost(6 * slots * tok * side * side, 10 * 2**20), name="front",
        )(slot_table, slot_table2, w_in, w_out, w_in2, w_out2, *ring)
        parts = lax.all_to_all(part, "tensor", 0, 0, axis_index_groups=y_groups, tiled=True)

        got, act2 = (lax.ppermute(v, "tensor", pair) for v in (sent, act))
        bins_shape = (n_dp, 2 * slots * per, side)
        pieces = pl.pallas_call(
            lambda *refs: bins_kernel(bin_scale, z_size, *refs),
            out_shape=(sds((z_size, 2 * slots * per, side), BF),) * x_size,
            in_specs=[free()] * 3 + [vm(), vm()], out_specs=(vm(),) * x_size,
            scratch_shapes=[
                pltpu.VMEM((blocks, 2, 2, half, side), BF), pltpu.VMEM(bins_shape, F32), pltpu.VMEM((2, cols, tok, side), BF),
                *index_scratch, dma(1), dma(2),
            ],
            compiler_params=params(VMEM_BINS), cost_estimate=cost(4 * slots * tok * side * side, 6 * 2**20), name="bins",
        )(slot_table, act, act2, kept, got)
        by_x = [pieces[0]]
        for d in range(1, x_size):
            by_x.append(lax.ppermute(pieces[d], "dp", [(p, (p + d * z_size) % n_dp) for p in range(n_dp)]))

        own = pl.pallas_call(
            rows_kernel, out_shape=sds((rows, width), BF), in_specs=[vm()], out_specs=vm(), compiler_params=params(),
            cost_estimate=cost(2**20, 2 * 2**20), name="rows",
        )(parts)
        near = [0, 1, x_size - 1]
        own, *tied = lax.optimization_barrier((own, *(by_x[d] for d in near)))
        for d, v in zip(near, tied):
            by_x[d] = v
        in_grad = lax.all_gather(own, "tensor", axis=0, tiled=True)
        in_grad = pl.pallas_call(
            place_kernel, out_shape=sds((tok, width), BF), in_specs=[hbm()], out_specs=hbm(),
            scratch_shapes=[pltpu.VMEM((tok, width), BF), dma(PARTS), dma(PARTS)],
            compiler_params=params(VMEM_FULL), cost_estimate=cost(0, 4 * 2**20), name="place",
        )(in_grad)

        stage = pl.pallas_call(
            stage_kernel, grid=(4,), out_shape=sds(by_x[0].shape, BF),
            in_specs=[pl.BlockSpec((z_size // 4, 2 * slots * per, side), lambda i: (i, 0, 0))] * x_size,
            out_specs=pl.BlockSpec((z_size // 4, 2 * slots * per, side), lambda i: (i, 0, 0)),
            compiler_params=params(), cost_estimate=cost(2**20, 2 * 2**20), name="stage",
        )(*by_x)
        sums = lax.all_to_all(stage, "dp", 0, 0, axis_index_groups=z_groups, tiled=True)
        win_grad, wout_grad = pl.pallas_call(
            lambda *refs: finish_kernel(bin_scale, *refs),
            out_shape=(sds((slots, per * side), F32), sds((slots, per * side), F32)),
            in_specs=[vm()], out_specs=(vm(), vm()),
            scratch_shapes=[pltpu.VMEM((2 * slots * per, side), F32)], compiler_params=params(), name="finish",
        )(sums)
        return in_grad, win_grad, wout_grad

    return local


def solution(mesh):
    z_size = 8
    in_specs = (
        P("dp", "tensor"),
        P("dp", "tensor"),
        P("tensor", None, None),
        P("tensor", None, None),
        P("tensor", None),
        P("tensor", None),
    )
    out_specs = (P("dp", None), P("tensor", "dp"), P("tensor", "dp"))
    return jax.shard_map(make_local(z_size), mesh=mesh, in_specs=in_specs, out_specs=out_specs, check_vma=False)
```

```python
import jax
import jax.numpy as jnp
from jax import lax
from jax.experimental import pallas as pl
from jax.experimental.pallas import tpu as pltpu
from jax.sharding import PartitionSpec as P

FF = 14336
CLIP = 4.0
LANES = 128
BF = jnp.bfloat16
F32 = jnp.float32
VMEM_LIMIT = 40 * 1024 * 1024
VMEM_FRONT = 48 * 1024 * 1024
VMEM_FETCH = 48 * 1024 * 1024
VMEM_BACK = 60 * 1024 * 1024
VMEM_BINS = 61 * 1024 * 1024
VMEM_FULL = 63 * 1024 * 1024
PARTS = 8


def dot(a, b, ca, cb):
    return lax.dot_general(a, b, (((ca,), (cb,)), ((), ())), preferred_element_type=F32)


def slot_index(rows_ref, cols_ref, s, dead_col):
    row = rows_ref[0, s]
    live = row >= 0
    return jnp.where(live, row, 0), jnp.where(live, cols_ref[0, s], dead_col)


def pack_kernel(ny, tok_ref, grad_ref, out_ref):
    tok = tok_ref.shape[0]
    rows = tok // (2 * ny)
    for k, ref in enumerate((tok_ref, grad_ref)):
        for h in range(2):
            for y in range(ny):
                val = ref[(2 * y + h) * rows : (2 * y + h + 1) * rows, :]
                for b in range(out_ref.shape[0]):
                    out_ref[b, k, h, y * rows : (y + 1) * rows, :] = val[:, b * LANES : (b + 1) * LANES]


def load_index(index_hbm, index_ref, sem):
    return [pltpu.make_async_copy(h, r, sem.at[k]) for k, (h, r) in enumerate(zip(index_hbm, index_ref))]


def run_all(copies):
    for c in copies:
        c.start()


def wait_all(copies):
    for c in copies:
        c.wait()


def own_core():
    return lax.rem(lax.axis_index("tensor"), 2)


def fetch_kernel(win_hbm, wout_hbm, win_ref, wout_ref, sems):
    copies = [pltpu.make_async_copy(win_hbm, win_ref, sems.at[0]), pltpu.make_async_copy(wout_hbm, wout_ref, sems.at[1])]
    run_all(copies)
    wait_all(copies)


def front_kernel(rows_hbm, cols_hbm, rows2_hbm, cols2_hbm, act_hbm, win1_ref, wout1_ref, win2_ref, wout2_ref,
                 out_hbm, mine_hbm, theirs_hbm, act_ref, pre_ref, dh_ref, acc_ref,
                 out_ref, mine_ref, theirs_ref, rows_ref, cols_ref, rows2_ref, cols2_ref, isems, sems, osems):
    slots = win1_ref.shape[0]
    col_count = pre_ref.shape[1] - 1
    index_copies = load_index(
        (rows_hbm, cols_hbm, rows2_hbm, cols2_hbm), (rows_ref, cols_ref, rows2_ref, cols2_ref), isems
    )
    run_all(index_copies)
    core = own_core()
    step = act_ref.shape[0] // PARTS
    copies = [pltpu.make_async_copy(act_hbm.at[pl.ds(k * step, step), :, core], act_ref.at[pl.ds(k * step, step)], sems.at[k])
              for k in range(PARTS)]
    win_ref, wout_ref = (win1_ref, win2_ref), (wout1_ref, wout2_ref)
    run_all(copies)
    pre_ref[...] = jnp.zeros_like(pre_ref)
    dh_ref[...] = jnp.zeros_like(dh_ref)
    acc_ref[...] = jnp.zeros_like(acc_ref)
    outs = (mine_ref, theirs_ref)
    for ref in outs:
        for k in range(2):
            ref[k, col_count] = jnp.zeros(ref.shape[2:], BF)
    wait_all(index_copies)
    index = [[slot_index(a, b, s, col_count) for s in range(slots)]
             for a, b in ((rows_ref, cols_ref), (rows2_ref, cols2_ref))]
    wait_all(copies)
    for k in range(2):
        for s in range(slots):
            r, c = index[k][s]
            pre_ref[k, c] += dot(act_ref[r, 0], win_ref[k][s], 1, 0)
            dh_ref[k, c] += dot(act_ref[r, 1], wout_ref[k][s], 1, 1)
    for k in (1, 0):
        for c in range(col_count):
            pre = pre_ref[k, c]
            sigma = jax.nn.sigmoid(pre)
            outs[k][0, c] = (dh_ref[k, c] * sigma * (1.0 + pre * (1.0 - sigma))).astype(BF)
            outs[k][1, c] = (pre * sigma).astype(BF)
    leaving = [pltpu.make_async_copy(theirs_ref, theirs_hbm, osems.at[0]), pltpu.make_async_copy(mine_ref, mine_hbm, osems.at[1])]
    run_all(leaving)
    for k in range(2):
        for s in range(slots):
            r, c = index[k][s]
            acc_ref[r] += dot(outs[k][0, c], win_ref[k][s], 1, 1)
    ny = out_ref.shape[0]
    rows = acc_ref.shape[1] // ny
    part = ny // 2
    for n in range(2):
        for b in range(acc_ref.shape[0]):
            val = acc_ref[b, n * part * rows : (n + 1) * part * rows, :].astype(BF)
            for y in range(part):
                out_ref[n * part + y, b * rows : (b + 1) * rows, :] = val[y * rows : (y + 1) * rows]
        at = pl.ds(n * part, part)
        leaving.append(pltpu.make_async_copy(out_ref.at[at], out_hbm.at[at], osems.at[2 + n]))
        leaving[-1].start()
    wait_all(leaving)


def bins_kernel(bin_scale, z_size, rows_hbm, cols_hbm, act_hbm, mine_ref, got_ref, *refs):
    n = len(refs) - 7
    bins_refs = refs[:n]
    act_ref, wide_ref, full_ref, rows_ref, cols_ref, isems, sems = refs[n:]
    slots = rows_ref.shape[1]
    groups = wide_ref.shape[0]
    per = LANES // groups
    half = mine_ref.shape[2]
    col_count = mine_ref.shape[1] - 1
    index_copies = load_index((rows_hbm, cols_hbm), (rows_ref, cols_ref), isems)
    step = act_ref.shape[0] // PARTS
    copies = [pltpu.make_async_copy(act_hbm.at[pl.ds(k * step, step)], act_ref.at[pl.ds(k * step, step)], sems.at[k])
              for k in range(PARTS)]
    run_all(index_copies)
    run_all(copies)
    core = own_core()
    for ref, first in ((mine_ref, core), (got_ref, 1 - core)):
        at = pl.ds(pl.multiple_of(first * half, half), half)
        for k in range(2):
            for c in range(col_count + 1):
                full_ref[k, c, at, :] = ref[k, c]
    wait_all(index_copies)
    index = [slot_index(rows_ref, cols_ref, s, col_count) for s in range(slots)]
    wait_all(copies)

    def put(val, slot):
        val = jnp.floor(jnp.clip(val, -CLIP, CLIP) * bin_scale)
        for g in range(groups):
            wide_ref[g, slot * per : (slot + 1) * per, :] = val[g * per : (g + 1) * per]

    for s in range(slots):
        r, c = index[s]
        put(dot(act_ref[r, 0].reshape(2 * half, LANES), full_ref[0, c], 0, 0), s)
        put(dot(full_ref[1, c], act_ref[r, 1].reshape(2 * half, LANES), 0, 0), slots + s)
    here = lax.axis_index("dp") // z_size
    for d in range(n):
        to = lax.rem(here + d, n)
        for z in range(z_size):
            bins_refs[d][z] = wide_ref[to * z_size + z].astype(BF)


def total_of(ref):
    total = ref[0].astype(F32)
    for k in range(1, ref.shape[0]):
        total += ref[k].astype(F32)
    return total


def rows_kernel(in_ref, out_ref):
    total = total_of(in_ref).astype(BF)
    rows, width = out_ref.shape
    for b in range(width // LANES):
        out_ref[:, b * LANES : (b + 1) * LANES] = total[b * rows : (b + 1) * rows]


def stage_kernel(*refs):
    total = refs[0][...].astype(F32)
    for ref in refs[1:-1]:
        total += ref[...].astype(F32)
    refs[-1][...] = total.astype(BF)


def place_kernel(in_ref, out_ref, buf_ref, in_sems, out_sems):
    parts = in_sems.shape[0]
    step = buf_ref.shape[0] // parts
    at = [pl.ds(k * step, step) for k in range(parts)]
    loads = [pltpu.make_async_copy(in_ref.at[at[k]], buf_ref.at[at[k]], in_sems.at[k]) for k in range(parts)]
    stores = [pltpu.make_async_copy(buf_ref.at[at[k]], out_ref.at[at[k]], out_sems.at[k]) for k in range(parts)]
    run_all(loads)
    for k in range(parts):
        loads[k].wait()
        stores[k].start()
    wait_all(stores)


def finish_kernel(bin_scale, in_ref, win_ref, wout_ref, wide_ref):
    slots = win_ref.shape[0]
    per = in_ref.shape[1] // (2 * slots)
    wide_ref[...] = total_of(in_ref) / bin_scale
    for j in range(per):
        at = slice(j * LANES, (j + 1) * LANES)
        win_ref[:, at] = wide_ref[pl.ds(j, slots, stride=per), :]
        wout_ref[:, at] = wide_ref[pl.ds(slots * per + j, slots, stride=per), :]


def vm():
    return pl.BlockSpec(memory_space=pltpu.VMEM)


def hbm():
    return pl.BlockSpec(memory_space=pltpu.HBM)


def sds(shape, dtype):
    return jax.ShapeDtypeStruct(shape, dtype)


def params(limit=VMEM_LIMIT):
    return pltpu.CompilerParams(vmem_limit_bytes=limit)


def cost(flops, nbytes):
    return pl.CostEstimate(flops=flops, bytes_accessed=nbytes, transcendentals=0)


def dma(n):
    return pltpu.SemaphoreType.DMA((n,))


def make_local(z_size):
    def local(tokens, out_grad, w_in, w_out, block_rows, block_cols):
        n_dp = lax.axis_size("dp")
        n_t = lax.axis_size("tensor")
        bin_scale = 4194304.0 / n_dp
        tok, feat = tokens.shape
        slots, side, _ = w_in.shape
        own_blocks = feat // side
        blocks = own_blocks * n_t
        width = blocks * side
        cols = FF // side // n_t + 1
        ny = n_t // 2
        x_size = n_dp // z_size
        rows = tok // n_t
        per = side // n_dp
        y_groups = [[2 * i + c for i in range(ny)] for c in range(2)]
        z_groups = [[z_size * i + j for j in range(z_size)] for i in range(x_size)]
        pair = [(i, i ^ 1) for i in range(n_t)]

        half = tok // 2
        packed = pl.pallas_call(
            lambda *refs: pack_kernel(ny, *refs), out_shape=sds((own_blocks, 2, 2, half, side), BF),
            in_specs=[vm(), vm()], out_specs=vm(), compiler_params=params(VMEM_FULL), name="pack",
        )(tokens, out_grad)
        act = lax.all_gather(packed.reshape(own_blocks * 2 * tok, side), "tensor", axis=0, tiled=True)
        act = act.reshape(blocks, 2, 2, half, side)
        weight = sds(w_in.shape, BF)
        w_in1, w_out1 = pl.pallas_call(
            fetch_kernel, out_shape=(weight, weight), in_specs=[hbm(), hbm()], out_specs=(vm(), vm()),
            scratch_shapes=[dma(2)], compiler_params=params(VMEM_FETCH), cost_estimate=cost(0, 4 * 2**20), name="fetch",
        )(w_in, w_out)
        swapped = [lax.ppermute(v, "tensor", pair) for v in (block_rows, block_cols, w_in, w_out)]
        act, w_in1, w_out1, *swapped = lax.optimization_barrier((act, w_in1, w_out1, *swapped))
        rows2, cols2, w_in2, w_out2 = swapped

        columns = sds((2, cols, half, side), BF)
        piece = sds((ny, blocks * rows, side), BF)
        index_scratch = [pltpu.SMEM(block_rows.shape, jnp.int32), pltpu.SMEM(block_cols.shape, jnp.int32)]
        part, kept, sent = pl.pallas_call(
            front_kernel, out_shape=(piece, columns, columns), in_specs=[hbm()] * 5 + [vm()] * 4, out_specs=(hbm(),) * 3,
            scratch_shapes=[
                pltpu.VMEM((blocks, 2, half, side), BF),
                pltpu.VMEM(columns.shape, F32), pltpu.VMEM(columns.shape, F32), pltpu.VMEM((blocks, half, side), F32),
                pltpu.VMEM(piece.shape, BF), pltpu.VMEM(columns.shape, BF), pltpu.VMEM(columns.shape, BF),
                *index_scratch, *index_scratch, dma(4), dma(PARTS), dma(4),
            ],
            compiler_params=params(VMEM_FRONT), cost_estimate=cost(6 * slots * tok * side * side, 10 * 2**20), name="front",
        )(block_rows, block_cols, rows2, cols2, act, w_in1, w_out1, w_in2, w_out2)
        parts = lax.all_to_all(part, "tensor", 0, 0, axis_index_groups=y_groups, tiled=True)

        got = lax.ppermute(sent, "tensor", pair)
        bins_shape = (n_dp, 2 * slots * per, side)
        pieces = pl.pallas_call(
            lambda *refs: bins_kernel(bin_scale, z_size, *refs),
            out_shape=(sds((z_size, 2 * slots * per, side), BF),) * x_size,
            in_specs=[hbm(), hbm(), hbm(), vm(), vm()], out_specs=(vm(),) * x_size,
            scratch_shapes=[
                pltpu.VMEM(act.shape, BF), pltpu.VMEM(bins_shape, F32), pltpu.VMEM((2, cols, tok, side), BF),
                *index_scratch, dma(2), dma(PARTS),
            ],
            compiler_params=params(VMEM_BINS), cost_estimate=cost(4 * slots * tok * side * side, 6 * 2**20), name="bins",
        )(block_rows, block_cols, act, kept, got)
        by_x = [pieces[0]]
        for d in range(1, x_size):
            by_x.append(lax.ppermute(pieces[d], "dp", [(p, (p + d * z_size) % n_dp) for p in range(n_dp)]))

        own = pl.pallas_call(
            rows_kernel, out_shape=sds((rows, width), BF), in_specs=[vm()], out_specs=vm(), compiler_params=params(),
            cost_estimate=cost(2**20, 2 * 2**20), name="rows",
        )(parts)
        near = [0, 1, x_size - 1]
        own, *tied = lax.optimization_barrier((own, *(by_x[d] for d in near)))
        for d, v in zip(near, tied):
            by_x[d] = v
        in_grad = lax.all_gather(own, "tensor", axis=0, tiled=True)
        in_grad = pl.pallas_call(
            place_kernel, out_shape=sds((tok, width), BF), in_specs=[hbm()], out_specs=hbm(),
            scratch_shapes=[pltpu.VMEM((tok, width), BF), dma(PARTS), dma(PARTS)],
            compiler_params=params(VMEM_FULL), cost_estimate=cost(0, 4 * 2**20), name="place",
        )(in_grad)

        stage = pl.pallas_call(
            stage_kernel, grid=(4,), out_shape=sds(by_x[0].shape, BF),
            in_specs=[pl.BlockSpec((z_size // 4, 2 * slots * per, side), lambda i: (i, 0, 0))] * x_size,
            out_specs=pl.BlockSpec((z_size // 4, 2 * slots * per, side), lambda i: (i, 0, 0)),
            compiler_params=params(), cost_estimate=cost(2**20, 2 * 2**20), name="stage",
        )(*by_x)
        sums = lax.all_to_all(stage, "dp", 0, 0, axis_index_groups=z_groups, tiled=True)
        win_grad, wout_grad = pl.pallas_call(
            lambda *refs: finish_kernel(bin_scale, *refs),
            out_shape=(sds((slots, per * side), F32), sds((slots, per * side), F32)),
            in_specs=[vm()], out_specs=(vm(), vm()),
            scratch_shapes=[pltpu.VMEM((2 * slots * per, side), F32)], compiler_params=params(), name="finish",
        )(sums)
        return in_grad, win_grad, wout_grad

    return local


def solution(mesh):
    z_size = 8
    in_specs = (
        P("dp", "tensor"),
        P("dp", "tensor"),
        P("tensor", None, None),
        P("tensor", None, None),
        P("tensor", None),
        P("tensor", None),
    )
    out_specs = (P("dp", None), P("tensor", "dp"), P("tensor", "dp"))
    return jax.shard_map(make_local(z_size), mesh=mesh, in_specs=in_specs, out_specs=out_specs, check_vma=False)
```

```python
import jax
import jax.numpy as jnp
from jax import lax
from jax.experimental import pallas as pl
from jax.experimental.pallas import tpu as pltpu
from jax.sharding import PartitionSpec as P

FF = 14336
CLIP = 4.0
LANES = 128
BF = jnp.bfloat16
F32 = jnp.float32
VMEM_LIMIT = 40 * 1024 * 1024
VMEM_FRONT = 49 * 1024 * 1024
VMEM_FETCH = 48 * 1024 * 1024
VMEM_BACK = 60 * 1024 * 1024
VMEM_BINS = 61 * 1024 * 1024
VMEM_FULL = 63 * 1024 * 1024
PARTS = 8


def dot(a, b, ca, cb):
    return lax.dot_general(a, b, (((ca,), (cb,)), ((), ())), preferred_element_type=F32)


def slot_index(rows_ref, cols_ref, s, dead_col):
    row = rows_ref[0, s]
    live = row >= 0
    return jnp.where(live, row, 0), jnp.where(live, cols_ref[0, s], dead_col)


def pack_kernel(ny, tok_ref, grad_ref, out_ref):
    tok = tok_ref.shape[0]
    rows = tok // (2 * ny)
    for k, ref in enumerate((tok_ref, grad_ref)):
        for h in range(2):
            for y in range(ny):
                val = ref[(2 * y + h) * rows : (2 * y + h + 1) * rows, :]
                for b in range(out_ref.shape[0]):
                    out_ref[b, k, h, y * rows : (y + 1) * rows, :] = val[:, b * LANES : (b + 1) * LANES]


def load_index(index_hbm, index_ref, sem):
    return [pltpu.make_async_copy(h, r, sem.at[k]) for k, (h, r) in enumerate(zip(index_hbm, index_ref))]


def run_all(copies):
    for c in copies:
        c.start()


def wait_all(copies):
    for c in copies:
        c.wait()


def own_core():
    return lax.rem(lax.axis_index("tensor"), 2)


def fetch_kernel(win_hbm, wout_hbm, win_ref, wout_ref, sems):
    copies = [pltpu.make_async_copy(win_hbm, win_ref, sems.at[0]), pltpu.make_async_copy(wout_hbm, wout_ref, sems.at[1])]
    run_all(copies)
    wait_all(copies)


def front_kernel(rows_hbm, cols_hbm, rows2_hbm, cols2_hbm, act_hbm, win1_ref, wout1_ref, win2_ref, wout2_ref,
                 out_hbm, both_hbm, act_ref, pre_ref, dh_ref, acc_ref,
                 out_ref, both_ref, rows_ref, cols_ref, rows2_ref, cols2_ref, isems, sems, osems):
    slots = win1_ref.shape[0]
    col_count = pre_ref.shape[1] - 1
    index_copies = load_index(
        (rows_hbm, cols_hbm, rows2_hbm, cols2_hbm), (rows_ref, cols_ref, rows2_ref, cols2_ref), isems
    )
    run_all(index_copies)
    core = own_core()
    step = act_ref.shape[0] // PARTS
    copies = [pltpu.make_async_copy(act_hbm.at[pl.ds(k * step, step), :, core], act_ref.at[pl.ds(k * step, step)], sems.at[k])
              for k in range(PARTS)]
    win_ref, wout_ref = (win1_ref, win2_ref), (wout1_ref, wout2_ref)
    run_all(copies)
    pre_ref[...] = jnp.zeros_like(pre_ref)
    dh_ref[...] = jnp.zeros_like(dh_ref)
    acc_ref[...] = jnp.zeros_like(acc_ref)
    for k in range(2):
        for n in range(2):
            both_ref[k, n, col_count] = jnp.zeros(both_ref.shape[3:], BF)
    wait_all(index_copies)
    index = [[slot_index(a, b, s, col_count) for s in range(slots)]
             for a, b in ((rows_ref, cols_ref), (rows2_ref, cols2_ref))]
    wait_all(copies)
    for k in range(2):
        for s in range(slots):
            r, c = index[k][s]
            pre_ref[k, c] += dot(act_ref[r, 0], win_ref[k][s], 1, 0)
            dh_ref[k, c] += dot(act_ref[r, 1], wout_ref[k][s], 1, 1)
    for k in (1, 0):
        for c in range(col_count):
            pre = pre_ref[k, c]
            sigma = jax.nn.sigmoid(pre)
            both_ref[k, 0, c] = (dh_ref[k, c] * sigma * (1.0 + pre * (1.0 - sigma))).astype(BF)
            both_ref[k, 1, c] = (pre * sigma).astype(BF)
    leaving = [pltpu.make_async_copy(both_ref, both_hbm, osems.at[2])]
    run_all(leaving)
    for k in range(2):
        for s in range(slots):
            r, c = index[k][s]
            acc_ref[r] += dot(both_ref[k, 0, c], win_ref[k][s], 1, 1)
    ny = out_ref.shape[0]
    rows = acc_ref.shape[1] // ny
    part = ny // 2
    for n in range(2):
        for b in range(acc_ref.shape[0]):
            val = acc_ref[b, n * part * rows : (n + 1) * part * rows, :].astype(BF)
            for y in range(part):
                out_ref[n * part + y, b * rows : (b + 1) * rows, :] = val[y * rows : (y + 1) * rows]
        at = pl.ds(n * part, part)
        leaving.append(pltpu.make_async_copy(out_ref.at[at], out_hbm.at[at], osems.at[n]))
        leaving[-1].start()
    wait_all(leaving)


def bins_kernel(bin_scale, z_size, rows_hbm, cols_hbm, act_hbm, both_ref, got_ref, *refs):
    n = len(refs) - 7
    bins_refs = refs[:n]
    act_ref, wide_ref, full_ref, rows_ref, cols_ref, isems, sems = refs[n:]
    slots = rows_ref.shape[1]
    groups = wide_ref.shape[0]
    per = LANES // groups
    half = got_ref.shape[2]
    col_count = got_ref.shape[1] - 1
    mine_ref = both_ref.at[0]
    index_copies = load_index((rows_hbm, cols_hbm), (rows_ref, cols_ref), isems)
    step = act_ref.shape[0] // PARTS
    copies = [pltpu.make_async_copy(act_hbm.at[pl.ds(k * step, step)], act_ref.at[pl.ds(k * step, step)], sems.at[k])
              for k in range(PARTS)]
    run_all(index_copies)
    run_all(copies)
    core = own_core()
    for ref, first in ((mine_ref, core), (got_ref, 1 - core)):
        at = pl.ds(pl.multiple_of(first * half, half), half)
        for k in range(2):
            for c in range(col_count + 1):
                full_ref[k, c, at, :] = ref[k, c]
    wait_all(index_copies)
    index = [slot_index(rows_ref, cols_ref, s, col_count) for s in range(slots)]
    wait_all(copies)

    def put(val, slot):
        val = jnp.floor(jnp.clip(val, -CLIP, CLIP) * bin_scale)
        for g in range(groups):
            wide_ref[g, slot * per : (slot + 1) * per, :] = val[g * per : (g + 1) * per]

    for s in range(slots):
        r, c = index[s]
        put(dot(act_ref[r, 0].reshape(2 * half, LANES), full_ref[0, c], 0, 0), s)
        put(dot(full_ref[1, c], act_ref[r, 1].reshape(2 * half, LANES), 0, 0), slots + s)
    here = lax.axis_index("dp") // z_size
    for d in range(n):
        to = lax.rem(here + d, n)
        for z in range(z_size):
            bins_refs[d][z] = wide_ref[to * z_size + z].astype(BF)


def total_of(ref):
    total = ref[0].astype(F32)
    for k in range(1, ref.shape[0]):
        total += ref[k].astype(F32)
    return total


def rows_kernel(in_ref, out_ref):
    total = total_of(in_ref).astype(BF)
    rows, width = out_ref.shape
    for b in range(width // LANES):
        out_ref[:, b * LANES : (b + 1) * LANES] = total[b * rows : (b + 1) * rows]


def stage_kernel(*refs):
    total = refs[0][...].astype(F32)
    for ref in refs[1:-1]:
        total += ref[...].astype(F32)
    refs[-1][...] = total.astype(BF)


def place_kernel(in_ref, out_ref, buf_ref, in_sems, out_sems):
    parts = in_sems.shape[0]
    step = buf_ref.shape[0] // parts
    at = [pl.ds(k * step, step) for k in range(parts)]
    loads = [pltpu.make_async_copy(in_ref.at[at[k]], buf_ref.at[at[k]], in_sems.at[k]) for k in range(parts)]
    stores = [pltpu.make_async_copy(buf_ref.at[at[k]], out_ref.at[at[k]], out_sems.at[k]) for k in range(parts)]
    run_all(loads)
    for k in range(parts):
        loads[k].wait()
        stores[k].start()
    wait_all(stores)


def finish_kernel(bin_scale, in_ref, win_ref, wout_ref, wide_ref):
    slots = win_ref.shape[0]
    per = in_ref.shape[1] // (2 * slots)
    wide_ref[...] = total_of(in_ref) / bin_scale
    for j in range(per):
        at = slice(j * LANES, (j + 1) * LANES)
        win_ref[:, at] = wide_ref[pl.ds(j, slots, stride=per), :]
        wout_ref[:, at] = wide_ref[pl.ds(slots * per + j, slots, stride=per), :]


def vm():
    return pl.BlockSpec(memory_space=pltpu.VMEM)


def hbm():
    return pl.BlockSpec(memory_space=pltpu.HBM)


def sds(shape, dtype):
    return jax.ShapeDtypeStruct(shape, dtype)


def params(limit=VMEM_LIMIT):
    return pltpu.CompilerParams(vmem_limit_bytes=limit)


def cost(flops, nbytes):
    return pl.CostEstimate(flops=flops, bytes_accessed=nbytes, transcendentals=0)


def dma(n):
    return pltpu.SemaphoreType.DMA((n,))


def make_local(z_size):
    def local(tokens, out_grad, w_in, w_out, block_rows, block_cols):
        n_dp = lax.axis_size("dp")
        n_t = lax.axis_size("tensor")
        bin_scale = 4194304.0 / n_dp
        tok, feat = tokens.shape
        slots, side, _ = w_in.shape
        own_blocks = feat // side
        blocks = own_blocks * n_t
        width = blocks * side
        cols = FF // side // n_t + 1
        ny = n_t // 2
        x_size = n_dp // z_size
        rows = tok // n_t
        per = side // n_dp
        y_groups = [[2 * i + c for i in range(ny)] for c in range(2)]
        z_groups = [[z_size * i + j for j in range(z_size)] for i in range(x_size)]
        pair = [(i, i ^ 1) for i in range(n_t)]

        half = tok // 2
        packed = pl.pallas_call(
            lambda *refs: pack_kernel(ny, *refs), out_shape=sds((own_blocks, 2, 2, half, side), BF),
            in_specs=[vm(), vm()], out_specs=vm(), compiler_params=params(VMEM_FULL), name="pack",
        )(tokens, out_grad)
        act = lax.all_gather(packed.reshape(own_blocks * 2 * tok, side), "tensor", axis=0, tiled=True)
        act = act.reshape(blocks, 2, 2, half, side)
        weight = sds(w_in.shape, BF)
        w_in1, w_out1 = pl.pallas_call(
            fetch_kernel, out_shape=(weight, weight), in_specs=[hbm(), hbm()], out_specs=(vm(), vm()),
            scratch_shapes=[dma(2)], compiler_params=params(VMEM_FETCH), cost_estimate=cost(0, 4 * 2**20), name="fetch",
        )(w_in, w_out)
        swapped = [lax.ppermute(v, "tensor", pair) for v in (block_rows, block_cols, w_in, w_out)]
        act, w_in1, w_out1, *swapped = lax.optimization_barrier((act, w_in1, w_out1, *swapped))
        rows2, cols2, w_in2, w_out2 = swapped

        columns = sds((2, cols, half, side), BF)
        piece = sds((ny, blocks * rows, side), BF)
        index_scratch = [pltpu.SMEM(block_rows.shape, jnp.int32), pltpu.SMEM(block_cols.shape, jnp.int32)]
        part, both = pl.pallas_call(
            front_kernel, out_shape=(piece, sds((2, *columns.shape), BF)), in_specs=[hbm()] * 5 + [vm()] * 4, out_specs=(hbm(), hbm()),
            scratch_shapes=[
                pltpu.VMEM((blocks, 2, half, side), BF),
                pltpu.VMEM(columns.shape, F32), pltpu.VMEM(columns.shape, F32), pltpu.VMEM((blocks, half, side), F32),
                pltpu.VMEM(piece.shape, BF), pltpu.VMEM((2, *columns.shape), BF),
                *index_scratch, *index_scratch, dma(4), dma(PARTS), dma(3),
            ],
            compiler_params=params(VMEM_FRONT), cost_estimate=cost(6 * slots * tok * side * side, 10 * 2**20), name="front",
        )(block_rows, block_cols, rows2, cols2, act, w_in1, w_out1, w_in2, w_out2)
        parts = lax.all_to_all(part, "tensor", 0, 0, axis_index_groups=y_groups, tiled=True)

        got = lax.ppermute(both[1], "tensor", pair)
        bins_shape = (n_dp, 2 * slots * per, side)
        pieces = pl.pallas_call(
            lambda *refs: bins_kernel(bin_scale, z_size, *refs),
            out_shape=(sds((z_size, 2 * slots * per, side), BF),) * x_size,
            in_specs=[hbm(), hbm(), hbm(), vm(), vm()], out_specs=(vm(),) * x_size,
            scratch_shapes=[
                pltpu.VMEM(act.shape, BF), pltpu.VMEM(bins_shape, F32), pltpu.VMEM((2, cols, tok, side), BF),
                *index_scratch, dma(2), dma(PARTS),
            ],
            compiler_params=params(VMEM_BINS), cost_estimate=cost(4 * slots * tok * side * side, 6 * 2**20), name="bins",
        )(block_rows, block_cols, act, both, got)
        by_x = [pieces[0]]
        for d in range(1, x_size):
            by_x.append(lax.ppermute(pieces[d], "dp", [(p, (p + d * z_size) % n_dp) for p in range(n_dp)]))

        own = pl.pallas_call(
            rows_kernel, out_shape=sds((rows, width), BF), in_specs=[vm()], out_specs=vm(), compiler_params=params(),
            cost_estimate=cost(2**20, 2 * 2**20), name="rows",
        )(parts)
        near = [0, 1, x_size - 1]
        own, *tied = lax.optimization_barrier((own, *(by_x[d] for d in near)))
        for d, v in zip(near, tied):
            by_x[d] = v
        in_grad = lax.all_gather(own, "tensor", axis=0, tiled=True)
        in_grad = pl.pallas_call(
            place_kernel, out_shape=sds((tok, width), BF), in_specs=[hbm()], out_specs=hbm(),
            scratch_shapes=[pltpu.VMEM((tok, width), BF), dma(PARTS), dma(PARTS)],
            compiler_params=params(VMEM_FULL), cost_estimate=cost(0, 4 * 2**20), name="place",
        )(in_grad)

        stage = pl.pallas_call(
            stage_kernel, grid=(4,), out_shape=sds(by_x[0].shape, BF),
            in_specs=[pl.BlockSpec((z_size // 4, 2 * slots * per, side), lambda i: (i, 0, 0))] * x_size,
            out_specs=pl.BlockSpec((z_size // 4, 2 * slots * per, side), lambda i: (i, 0, 0)),
            compiler_params=params(), cost_estimate=cost(2**20, 2 * 2**20), name="stage",
        )(*by_x)
        sums = lax.all_to_all(stage, "dp", 0, 0, axis_index_groups=z_groups, tiled=True)
        win_grad, wout_grad = pl.pallas_call(
            lambda *refs: finish_kernel(bin_scale, *refs),
            out_shape=(sds((slots, per * side), F32), sds((slots, per * side), F32)),
            in_specs=[vm()], out_specs=(vm(), vm()),
            scratch_shapes=[pltpu.VMEM((2 * slots * per, side), F32)], compiler_params=params(), name="finish",
        )(sums)
        return in_grad, win_grad, wout_grad

    return local


def solution(mesh):
    z_size = 8
    in_specs = (
        P("dp", "tensor"),
        P("dp", "tensor"),
        P("tensor", None, None),
        P("tensor", None, None),
        P("tensor", None),
        P("tensor", None),
    )
    out_specs = (P("dp", None), P("tensor", "dp"), P("tensor", "dp"))
    return jax.shard_map(make_local(z_size), mesh=mesh, in_specs=in_specs, out_specs=out_specs, check_vma=False)
```

```python
import jax
import jax.numpy as jnp
from jax import lax
from jax.experimental import pallas as pl
from jax.experimental.pallas import tpu as pltpu
from jax.sharding import PartitionSpec as P

FF = 14336
CLIP = 4.0
LANES = 128
BF = jnp.bfloat16
F32 = jnp.float32
VMEM_LIMIT = 40 * 1024 * 1024
VMEM_FRONT = 49 * 1024 * 1024
VMEM_FETCH = 48 * 1024 * 1024
VMEM_BACK = 60 * 1024 * 1024
VMEM_BINS = 61 * 1024 * 1024
VMEM_FULL = 63 * 1024 * 1024
PARTS = 8


def dot(a, b, ca, cb):
    return lax.dot_general(a, b, (((ca,), (cb,)), ((), ())), preferred_element_type=F32)


def slot_index(rows_ref, cols_ref, s, dead_col):
    row = rows_ref[0, s]
    live = row >= 0
    return jnp.where(live, row, 0), jnp.where(live, cols_ref[0, s], dead_col)


def pack_kernel(ny, tok_ref, grad_ref, out_ref):
    tok = tok_ref.shape[0]
    rows = tok // (2 * ny)
    for k, ref in enumerate((tok_ref, grad_ref)):
        for h in range(2):
            for y in range(ny):
                val = ref[(2 * y + h) * rows : (2 * y + h + 1) * rows, :]
                for b in range(out_ref.shape[0]):
                    out_ref[b, k, h, y * rows : (y + 1) * rows, :] = val[:, b * LANES : (b + 1) * LANES]


def load_index(index_hbm, index_ref, sem):
    return [pltpu.make_async_copy(h, r, sem.at[k]) for k, (h, r) in enumerate(zip(index_hbm, index_ref))]


def run_all(copies):
    for c in copies:
        c.start()


def wait_all(copies):
    for c in copies:
        c.wait()


def own_core():
    return lax.rem(lax.axis_index("tensor"), 2)


def fetch_kernel(win_hbm, wout_hbm, win_ref, wout_ref, sems):
    copies = [pltpu.make_async_copy(win_hbm, win_ref, sems.at[0]), pltpu.make_async_copy(wout_hbm, wout_ref, sems.at[1])]
    run_all(copies)
    wait_all(copies)


def front_kernel(rows_hbm, cols_hbm, rows2_hbm, cols2_hbm, act_hbm, win1_ref, wout1_ref, win2_ref, wout2_ref,
                 out_hbm, both_hbm, act_ref, pre_ref, dh_ref, acc_ref,
                 out_ref, both_ref, rows_ref, cols_ref, rows2_ref, cols2_ref, isems, sems, osems):
    slots = win1_ref.shape[0]
    col_count = pre_ref.shape[1] - 1
    index_copies = load_index(
        (rows_hbm, cols_hbm, rows2_hbm, cols2_hbm), (rows_ref, cols_ref, rows2_ref, cols2_ref), isems
    )
    run_all(index_copies)
    core = own_core()
    step = act_ref.shape[0] // PARTS
    copies = [pltpu.make_async_copy(act_hbm.at[pl.ds(k * step, step), :, core], act_ref.at[pl.ds(k * step, step)], sems.at[k])
              for k in range(PARTS)]
    win_ref, wout_ref = (win1_ref, win2_ref), (wout1_ref, wout2_ref)
    run_all(copies)
    pre_ref[...] = jnp.zeros_like(pre_ref)
    dh_ref[...] = jnp.zeros_like(dh_ref)
    acc_ref[...] = jnp.zeros_like(acc_ref)
    for k in range(2):
        for n in range(2):
            both_ref[k, n, col_count] = jnp.zeros(both_ref.shape[3:], BF)
    wait_all(index_copies)
    index = [[slot_index(a, b, s, col_count) for s in range(slots)]
             for a, b in ((rows_ref, cols_ref), (rows2_ref, cols2_ref))]
    wait_all(copies)
    for k in (1, 0):
        for s in range(slots):
            r, c = index[k][s]
            pre_ref[k, c] += dot(act_ref[r, 0], win_ref[k][s], 1, 0)
            dh_ref[k, c] += dot(act_ref[r, 1], wout_ref[k][s], 1, 1)
        for c in range(col_count):
            pre = pre_ref[k, c]
            sigma = jax.nn.sigmoid(pre)
            both_ref[k, 0, c] = (dh_ref[k, c] * sigma * (1.0 + pre * (1.0 - sigma))).astype(BF)
            both_ref[k, 1, c] = (pre * sigma).astype(BF)
    leaving = [pltpu.make_async_copy(both_ref, both_hbm, osems.at[2])]
    run_all(leaving)
    for k in (1, 0):
        for s in range(slots):
            r, c = index[k][s]
            acc_ref[r] += dot(both_ref[k, 0, c], win_ref[k][s], 1, 1)
    ny = out_ref.shape[0]
    rows = acc_ref.shape[1] // ny
    part = ny // 2
    for n in range(2):
        for b in range(acc_ref.shape[0]):
            val = acc_ref[b, n * part * rows : (n + 1) * part * rows, :].astype(BF)
            for y in range(part):
                out_ref[n * part + y, b * rows : (b + 1) * rows, :] = val[y * rows : (y + 1) * rows]
        at = pl.ds(n * part, part)
        leaving.append(pltpu.make_async_copy(out_ref.at[at], out_hbm.at[at], osems.at[n]))
        leaving[-1].start()
    wait_all(leaving)


def bins_kernel(bin_scale, z_size, rows_hbm, cols_hbm, act_hbm, both_ref, got_ref, *refs):
    n = len(refs) - 7
    bins_refs = refs[:n]
    act_ref, wide_ref, full_ref, rows_ref, cols_ref, isems, sems = refs[n:]
    slots = rows_ref.shape[1]
    groups = wide_ref.shape[0]
    per = LANES // groups
    half = got_ref.shape[2]
    col_count = got_ref.shape[1] - 1
    mine_ref = both_ref.at[0]
    index_copies = load_index((rows_hbm, cols_hbm), (rows_ref, cols_ref), isems)
    step = act_ref.shape[0] // PARTS
    copies = [pltpu.make_async_copy(act_hbm.at[pl.ds(k * step, step)], act_ref.at[pl.ds(k * step, step)], sems.at[k])
              for k in range(PARTS)]
    run_all(index_copies)
    run_all(copies)
    core = own_core()
    for ref, first in ((mine_ref, core), (got_ref, 1 - core)):
        at = pl.ds(pl.multiple_of(first * half, half), half)
        for k in range(2):
            for c in range(col_count + 1):
                full_ref[k, c, at, :] = ref[k, c]
    wait_all(index_copies)
    index = [slot_index(rows_ref, cols_ref, s, col_count) for s in range(slots)]
    wait_all(copies)

    def put(val, slot):
        val = jnp.floor(jnp.clip(val, -CLIP, CLIP) * bin_scale)
        for g in range(groups):
            wide_ref[g, slot * per : (slot + 1) * per, :] = val[g * per : (g + 1) * per]

    for s in range(slots):
        r, c = index[s]
        put(dot(act_ref[r, 0].reshape(2 * half, LANES), full_ref[0, c], 0, 0), s)
        put(dot(full_ref[1, c], act_ref[r, 1].reshape(2 * half, LANES), 0, 0), slots + s)
    here = lax.axis_index("dp") // z_size
    for d in range(n):
        to = lax.rem(here + d, n)
        for z in range(z_size):
            bins_refs[d][z] = wide_ref[to * z_size + z].astype(BF)


def total_of(ref):
    total = ref[0].astype(F32)
    for k in range(1, ref.shape[0]):
        total += ref[k].astype(F32)
    return total


def rows_kernel(in_ref, out_ref):
    total = total_of(in_ref).astype(BF)
    rows, width = out_ref.shape
    for b in range(width // LANES):
        out_ref[:, b * LANES : (b + 1) * LANES] = total[b * rows : (b + 1) * rows]


def stage_kernel(*refs):
    total = refs[0][...].astype(F32)
    for ref in refs[1:-1]:
        total += ref[...].astype(F32)
    refs[-1][...] = total.astype(BF)


def place_kernel(in_ref, out_ref, buf_ref, in_sems, out_sems):
    parts = in_sems.shape[0]
    step = buf_ref.shape[0] // parts
    at = [pl.ds(k * step, step) for k in range(parts)]
    loads = [pltpu.make_async_copy(in_ref.at[at[k]], buf_ref.at[at[k]], in_sems.at[k]) for k in range(parts)]
    stores = [pltpu.make_async_copy(buf_ref.at[at[k]], out_ref.at[at[k]], out_sems.at[k]) for k in range(parts)]
    run_all(loads)
    for k in range(parts):
        loads[k].wait()
        stores[k].start()
    wait_all(stores)


def finish_kernel(bin_scale, in_ref, win_ref, wout_ref, wide_ref):
    slots = win_ref.shape[0]
    per = in_ref.shape[1] // (2 * slots)
    wide_ref[...] = total_of(in_ref) / bin_scale
    for j in range(per):
        at = slice(j * LANES, (j + 1) * LANES)
        win_ref[:, at] = wide_ref[pl.ds(j, slots, stride=per), :]
        wout_ref[:, at] = wide_ref[pl.ds(slots * per + j, slots, stride=per), :]


def vm():
    return pl.BlockSpec(memory_space=pltpu.VMEM)


def hbm():
    return pl.BlockSpec(memory_space=pltpu.HBM)


def sds(shape, dtype):
    return jax.ShapeDtypeStruct(shape, dtype)


def params(limit=VMEM_LIMIT):
    return pltpu.CompilerParams(vmem_limit_bytes=limit)


def cost(flops, nbytes):
    return pl.CostEstimate(flops=flops, bytes_accessed=nbytes, transcendentals=0)


def dma(n):
    return pltpu.SemaphoreType.DMA((n,))


def make_local(z_size):
    def local(tokens, out_grad, w_in, w_out, block_rows, block_cols):
        n_dp = lax.axis_size("dp")
        n_t = lax.axis_size("tensor")
        bin_scale = 4194304.0 / n_dp
        tok, feat = tokens.shape
        slots, side, _ = w_in.shape
        own_blocks = feat // side
        blocks = own_blocks * n_t
        width = blocks * side
        cols = FF // side // n_t + 1
        ny = n_t // 2
        x_size = n_dp // z_size
        rows = tok // n_t
        per = side // n_dp
        y_groups = [[2 * i + c for i in range(ny)] for c in range(2)]
        z_groups = [[z_size * i + j for j in range(z_size)] for i in range(x_size)]
        pair = [(i, i ^ 1) for i in range(n_t)]

        half = tok // 2
        packed = pl.pallas_call(
            lambda *refs: pack_kernel(ny, *refs), out_shape=sds((own_blocks, 2, 2, half, side), BF),
            in_specs=[vm(), vm()], out_specs=vm(), compiler_params=params(VMEM_FULL), name="pack",
        )(tokens, out_grad)
        act = lax.all_gather(packed.reshape(own_blocks * 2 * tok, side), "tensor", axis=0, tiled=True)
        act = act.reshape(blocks, 2, 2, half, side)
        weight = sds(w_in.shape, BF)
        w_in1, w_out1 = pl.pallas_call(
            fetch_kernel, out_shape=(weight, weight), in_specs=[hbm(), hbm()], out_specs=(vm(), vm()),
            scratch_shapes=[dma(2)], compiler_params=params(VMEM_FETCH), cost_estimate=cost(0, 4 * 2**20), name="fetch",
        )(w_in, w_out)
        swapped = [lax.ppermute(v, "tensor", pair) for v in (block_rows, block_cols, w_in, w_out)]
        act, w_in1, w_out1, *swapped = lax.optimization_barrier((act, w_in1, w_out1, *swapped))
        rows2, cols2, w_in2, w_out2 = swapped

        columns = sds((2, cols, half, side), BF)
        piece = sds((ny, blocks * rows, side), BF)
        index_scratch = [pltpu.SMEM(block_rows.shape, jnp.int32), pltpu.SMEM(block_cols.shape, jnp.int32)]
        part, both = pl.pallas_call(
            front_kernel, out_shape=(piece, sds((2, *columns.shape), BF)), in_specs=[hbm()] * 5 + [vm()] * 4, out_specs=(hbm(), hbm()),
            scratch_shapes=[
                pltpu.VMEM((blocks, 2, half, side), BF),
                pltpu.VMEM(columns.shape, F32), pltpu.VMEM(columns.shape, F32), pltpu.VMEM((blocks, half, side), F32),
                pltpu.VMEM(piece.shape, BF), pltpu.VMEM((2, *columns.shape), BF),
                *index_scratch, *index_scratch, dma(4), dma(PARTS), dma(3),
            ],
            compiler_params=params(VMEM_FRONT), cost_estimate=cost(6 * slots * tok * side * side, 10 * 2**20), name="front",
        )(block_rows, block_cols, rows2, cols2, act, w_in1, w_out1, w_in2, w_out2)
        parts = lax.all_to_all(part, "tensor", 0, 0, axis_index_groups=y_groups, tiled=True)

        got = lax.ppermute(both[1], "tensor", pair)
        bins_shape = (n_dp, 2 * slots * per, side)
        pieces = pl.pallas_call(
            lambda *refs: bins_kernel(bin_scale, z_size, *refs),
            out_shape=(sds((z_size, 2 * slots * per, side), BF),) * x_size,
            in_specs=[hbm(), hbm(), hbm(), vm(), vm()], out_specs=(vm(),) * x_size,
            scratch_shapes=[
                pltpu.VMEM(act.shape, BF), pltpu.VMEM(bins_shape, F32), pltpu.VMEM((2, cols, tok, side), BF),
                *index_scratch, dma(2), dma(PARTS),
            ],
            compiler_params=params(VMEM_BINS), cost_estimate=cost(4 * slots * tok * side * side, 6 * 2**20), name="bins",
        )(block_rows, block_cols, act, both, got)
        by_x = [pieces[0]]
        for d in range(1, x_size):
            by_x.append(lax.ppermute(pieces[d], "dp", [(p, (p + d * z_size) % n_dp) for p in range(n_dp)]))

        own = pl.pallas_call(
            rows_kernel, out_shape=sds((rows, width), BF), in_specs=[vm()], out_specs=vm(), compiler_params=params(),
            cost_estimate=cost(2**20, 2 * 2**20), name="rows",
        )(parts)
        near = [0, 1, x_size - 1]
        own, *tied = lax.optimization_barrier((own, *(by_x[d] for d in near)))
        for d, v in zip(near, tied):
            by_x[d] = v
        in_grad = lax.all_gather(own, "tensor", axis=0, tiled=True)
        in_grad = pl.pallas_call(
            place_kernel, out_shape=sds((tok, width), BF), in_specs=[hbm()], out_specs=hbm(),
            scratch_shapes=[pltpu.VMEM((tok, width), BF), dma(PARTS), dma(PARTS)],
            compiler_params=params(VMEM_FULL), cost_estimate=cost(0, 4 * 2**20), name="place",
        )(in_grad)

        stage = pl.pallas_call(
            stage_kernel, grid=(4,), out_shape=sds(by_x[0].shape, BF),
            in_specs=[pl.BlockSpec((z_size // 4, 2 * slots * per, side), lambda i: (i, 0, 0))] * x_size,
            out_specs=pl.BlockSpec((z_size // 4, 2 * slots * per, side), lambda i: (i, 0, 0)),
            compiler_params=params(), cost_estimate=cost(2**20, 2 * 2**20), name="stage",
        )(*by_x)
        sums = lax.all_to_all(stage, "dp", 0, 0, axis_index_groups=z_groups, tiled=True)
        win_grad, wout_grad = pl.pallas_call(
            lambda *refs: finish_kernel(bin_scale, *refs),
            out_shape=(sds((slots, per * side), F32), sds((slots, per * side), F32)),
            in_specs=[vm()], out_specs=(vm(), vm()),
            scratch_shapes=[pltpu.VMEM((2 * slots * per, side), F32)], compiler_params=params(), name="finish",
        )(sums)
        return in_grad, win_grad, wout_grad

    return local


def solution(mesh):
    z_size = 8
    in_specs = (
        P("dp", "tensor"),
        P("dp", "tensor"),
        P("tensor", None, None),
        P("tensor", None, None),
        P("tensor", None),
        P("tensor", None),
    )
    out_specs = (P("dp", None), P("tensor", "dp"), P("tensor", "dp"))
    return jax.shard_map(make_local(z_size), mesh=mesh, in_specs=in_specs, out_specs=out_specs, check_vma=False)
```

```python
import jax
import jax.numpy as jnp
from jax import lax
from jax.experimental import pallas as pl
from jax.experimental.pallas import tpu as pltpu
from jax.sharding import PartitionSpec as P

FF = 14336
CLIP = 4.0
LANES = 128
BF = jnp.bfloat16
F32 = jnp.float32
VMEM_LIMIT = 40 * 1024 * 1024
VMEM_FRONT = 49 * 1024 * 1024
VMEM_FETCH = 48 * 1024 * 1024
VMEM_BACK = 60 * 1024 * 1024
VMEM_BINS = 61 * 1024 * 1024
VMEM_FULL = 63 * 1024 * 1024
PARTS = 8


def dot(a, b, ca, cb):
    return lax.dot_general(a, b, (((ca,), (cb,)), ((), ())), preferred_element_type=F32)


def slot_index(rows_ref, cols_ref, s, dead_col):
    row = rows_ref[0, s]
    live = row >= 0
    return jnp.where(live, row, 0), jnp.where(live, cols_ref[0, s], dead_col)


def pack_kernel(ny, tok_ref, grad_ref, out_ref):
    tok = tok_ref.shape[0]
    rows = tok // (2 * ny)
    for k, ref in enumerate((tok_ref, grad_ref)):
        for h in range(2):
            for y in range(ny):
                val = ref[(2 * y + h) * rows : (2 * y + h + 1) * rows, :]
                for b in range(out_ref.shape[0]):
                    out_ref[b, k, h, y * rows : (y + 1) * rows, :] = val[:, b * LANES : (b + 1) * LANES]


def load_index(index_hbm, index_ref, sem):
    return [pltpu.make_async_copy(h, r, sem.at[k]) for k, (h, r) in enumerate(zip(index_hbm, index_ref))]


def run_all(copies):
    for c in copies:
        c.start()


def wait_all(copies):
    for c in copies:
        c.wait()


def own_core():
    return lax.rem(lax.axis_index("tensor"), 2)


def fetch_kernel(win_hbm, wout_hbm, win_ref, wout_ref, sems):
    copies = [pltpu.make_async_copy(win_hbm, win_ref, sems.at[0]), pltpu.make_async_copy(wout_hbm, wout_ref, sems.at[1])]
    run_all(copies)
    wait_all(copies)


def front_kernel(rows_hbm, cols_hbm, rows2_hbm, cols2_hbm, act_hbm, win1_ref, wout1_ref, win2_ref, wout2_ref,
                 out_hbm, both_hbm, act_ref, pre_ref, dh_ref, acc_ref,
                 out_ref, both_ref, rows_ref, cols_ref, rows2_ref, cols2_ref, isems, sems, osems):
    slots = win1_ref.shape[0]
    col_count = pre_ref.shape[1] - 1
    index_copies = load_index(
        (rows_hbm, cols_hbm, rows2_hbm, cols2_hbm), (rows_ref, cols_ref, rows2_ref, cols2_ref), isems
    )
    run_all(index_copies)
    core = own_core()
    step = act_ref.shape[0] // PARTS
    copies = [pltpu.make_async_copy(act_hbm.at[pl.ds(k * step, step), :, core], act_ref.at[pl.ds(k * step, step)], sems.at[k])
              for k in range(PARTS)]
    win_ref, wout_ref = (win1_ref, win2_ref), (wout1_ref, wout2_ref)
    run_all(copies)
    pre_ref[...] = jnp.zeros_like(pre_ref)
    dh_ref[...] = jnp.zeros_like(dh_ref)
    acc_ref[...] = jnp.zeros_like(acc_ref)
    for k in range(2):
        for n in range(2):
            both_ref[k, n, col_count] = jnp.zeros(both_ref.shape[3:], BF)
    wait_all(index_copies)
    index = [[slot_index(a, b, s, col_count) for s in range(slots)]
             for a, b in ((rows_ref, cols_ref), (rows2_ref, cols2_ref))]
    wait_all(copies)
    for k in range(2):
        for s in range(slots):
            r, c = index[k][s]
            pre_ref[k, c] += dot(act_ref[r, 0], win_ref[k][s], 1, 0)
            dh_ref[k, c] += dot(act_ref[r, 1], wout_ref[k][s], 1, 1)
    for k in (1, 0):
        for c in range(col_count):
            pre = pre_ref[k, c]
            sigma = jax.nn.sigmoid(pre)
            both_ref[k, 0, c] = (dh_ref[k, c] * sigma * (1.0 + pre * (1.0 - sigma))).astype(BF)
            both_ref[k, 1, c] = (pre * sigma).astype(BF)
    leaving = [pltpu.make_async_copy(both_ref, both_hbm, osems.at[2])]
    run_all(leaving)
    for k in range(2):
        for s in range(slots):
            r, c = index[k][s]
            acc_ref[r] += dot(both_ref[k, 0, c], win_ref[k][s], 1, 1)
    ny = out_ref.shape[0]
    rows = acc_ref.shape[1] // ny
    part = ny // 2
    for n in range(2):
        for b in range(acc_ref.shape[0]):
            val = acc_ref[b, n * part * rows : (n + 1) * part * rows, :].astype(BF)
            for y in range(part):
                out_ref[n * part + y, b * rows : (b + 1) * rows, :] = val[y * rows : (y + 1) * rows]
        at = pl.ds(n * part, part)
        leaving.append(pltpu.make_async_copy(out_ref.at[at], out_hbm.at[at], osems.at[n]))
        leaving[-1].start()
    wait_all(leaving)


def bins_kernel(bin_scale, z_size, rows_hbm, cols_hbm, act_hbm, both_ref, got_ref, *refs):
    n = len(refs) - 7
    bins_refs = refs[:n]
    act_ref, wide_ref, full_ref, rows_ref, cols_ref, isems, sems = refs[n:]
    slots = rows_ref.shape[1]
    groups = wide_ref.shape[0]
    per = LANES // groups
    half = got_ref.shape[2]
    col_count = got_ref.shape[1] - 1
    mine_ref = both_ref.at[0]
    index_copies = load_index((rows_hbm, cols_hbm), (rows_ref, cols_ref), isems)
    step = act_ref.shape[0] // PARTS
    copies = [pltpu.make_async_copy(act_hbm.at[pl.ds(k * step, step)], act_ref.at[pl.ds(k * step, step)], sems.at[k])
              for k in range(PARTS)]
    run_all(index_copies)
    run_all(copies)
    core = own_core()
    for ref, first in ((mine_ref, core), (got_ref, 1 - core)):
        at = pl.ds(pl.multiple_of(first * half, half), half)
        for k in range(2):
            for c in range(col_count + 1):
                full_ref[k, c, at, :] = ref[k, c]
    wait_all(index_copies)
    index = [slot_index(rows_ref, cols_ref, s, col_count) for s in range(slots)]
    wait_all(copies)

    def put(val, slot):
        val = jnp.floor(jnp.clip(val, -CLIP, CLIP) * bin_scale)
        for g in range(groups):
            wide_ref[g, slot * per : (slot + 1) * per, :] = val[g * per : (g + 1) * per]

    for s in range(slots):
        r, c = index[s]
        put(dot(act_ref[r, 0].reshape(2 * half, LANES), full_ref[0, c], 0, 0), s)
        put(dot(full_ref[1, c], act_ref[r, 1].reshape(2 * half, LANES), 0, 0), slots + s)
    here = lax.axis_index("dp") // z_size
    for d in range(n):
        to = lax.rem(here + d, n)
        for z in range(z_size):
            bins_refs[d][z] = wide_ref[to * z_size + z].astype(BF)


def total_of(ref):
    total = ref[0].astype(F32)
    for k in range(1, ref.shape[0]):
        total += ref[k].astype(F32)
    return total


def rows_kernel(in_ref, out_ref):
    total = total_of(in_ref).astype(BF)
    rows, width = out_ref.shape
    for b in range(width // LANES):
        out_ref[:, b * LANES : (b + 1) * LANES] = total[b * rows : (b + 1) * rows]


def stage_kernel(*refs):
    total = refs[0][...].astype(F32)
    for ref in refs[1:-1]:
        total += ref[...].astype(F32)
    refs[-1][...] = total.astype(BF)


def place_kernel(in_ref, out_ref, buf_ref, in_sems, out_sems):
    parts = in_sems.shape[0]
    step = buf_ref.shape[0] // parts
    at = [pl.ds(k * step, step) for k in range(parts)]
    loads = [pltpu.make_async_copy(in_ref.at[at[k]], buf_ref.at[at[k]], in_sems.at[k]) for k in range(parts)]
    stores = [pltpu.make_async_copy(buf_ref.at[at[k]], out_ref.at[at[k]], out_sems.at[k]) for k in range(parts)]
    run_all(loads)
    for k in range(parts):
        loads[k].wait()
        stores[k].start()
    wait_all(stores)


def finish_kernel(bin_scale, in_ref, win_ref, wout_ref, wide_ref):
    slots = win_ref.shape[0]
    per = in_ref.shape[1] // (2 * slots)
    wide_ref[...] = total_of(in_ref) / bin_scale
    for j in range(per):
        at = slice(j * LANES, (j + 1) * LANES)
        win_ref[:, at] = wide_ref[pl.ds(j, slots, stride=per), :]
        wout_ref[:, at] = wide_ref[pl.ds(slots * per + j, slots, stride=per), :]


def vm():
    return pl.BlockSpec(memory_space=pltpu.VMEM)


def hbm():
    return pl.BlockSpec(memory_space=pltpu.HBM)


def sds(shape, dtype):
    return jax.ShapeDtypeStruct(shape, dtype)


def params(limit=VMEM_LIMIT):
    return pltpu.CompilerParams(vmem_limit_bytes=limit)


def cost(flops, nbytes):
    return pl.CostEstimate(flops=flops, bytes_accessed=nbytes, transcendentals=0)


def dma(n):
    return pltpu.SemaphoreType.DMA((n,))


def make_local(z_size):
    def local(tokens, out_grad, w_in, w_out, block_rows, block_cols):
        n_dp = lax.axis_size("dp")
        n_t = lax.axis_size("tensor")
        bin_scale = 4194304.0 / n_dp
        tok, feat = tokens.shape
        slots, side, _ = w_in.shape
        own_blocks = feat // side
        blocks = own_blocks * n_t
        width = blocks * side
        cols = FF // side // n_t + 1
        ny = n_t // 2
        x_size = n_dp // z_size
        rows = tok // n_t
        per = side // n_dp
        y_groups = [[2 * i + c for i in range(ny)] for c in range(2)]
        z_groups = [[z_size * i + j for j in range(z_size)] for i in range(x_size)]
        pair = [(i, i ^ 1) for i in range(n_t)]

        half = tok // 2
        packed = pl.pallas_call(
            lambda *refs: pack_kernel(ny, *refs), out_shape=sds((own_blocks, 2, 2, half, side), BF),
            in_specs=[vm(), vm()], out_specs=vm(), compiler_params=params(VMEM_FULL), name="pack",
        )(tokens, out_grad)
        act = lax.all_gather(packed.reshape(own_blocks * 2 * tok, side), "tensor", axis=0, tiled=True)
        act = act.reshape(blocks, 2, 2, half, side)
        weight = sds(w_in.shape, BF)
        w_in1, w_out1 = pl.pallas_call(
            fetch_kernel, out_shape=(weight, weight), in_specs=[hbm(), hbm()], out_specs=(vm(), vm()),
            scratch_shapes=[dma(2)], compiler_params=params(VMEM_FETCH), cost_estimate=cost(0, 4 * 2**20), name="fetch",
        )(w_in, w_out)
        swapped = [lax.ppermute(v, "tensor", pair) for v in (block_rows, block_cols, w_in, w_out)]
        act, w_in1, w_out1, *swapped = lax.optimization_barrier((act, w_in1, w_out1, *swapped))
        rows2, cols2, w_in2, w_out2 = swapped

        columns = sds((2, cols, half, side), BF)
        piece = sds((ny, blocks * rows, side), BF)
        index_scratch = [pltpu.SMEM(block_rows.shape, jnp.int32), pltpu.SMEM(block_cols.shape, jnp.int32)]
        part, both = pl.pallas_call(
            front_kernel, out_shape=(piece, sds((2, *columns.shape), BF)), in_specs=[hbm()] * 5 + [vm()] * 4, out_specs=(hbm(), hbm()),
            scratch_shapes=[
                pltpu.VMEM((blocks, 2, half, side), BF),
                pltpu.VMEM(columns.shape, F32), pltpu.VMEM(columns.shape, F32), pltpu.VMEM((blocks, half, side), F32),
                pltpu.VMEM(piece.shape, BF), pltpu.VMEM((2, *columns.shape), BF),
                *index_scratch, *index_scratch, dma(4), dma(PARTS), dma(3),
            ],
            compiler_params=params(VMEM_FRONT), cost_estimate=cost(6 * slots * tok * side * side, 10 * 2**20), name="front",
        )(block_rows, block_cols, rows2, cols2, act, w_in1, w_out1, w_in2, w_out2)
        parts = lax.all_to_all(part, "tensor", 0, 0, axis_index_groups=y_groups, tiled=True)

        got = lax.ppermute(both[1], "tensor", pair)
        bins_shape = (n_dp, 2 * slots * per, side)
        pieces = pl.pallas_call(
            lambda *refs: bins_kernel(bin_scale, z_size, *refs),
            out_shape=(sds((z_size, 2 * slots * per, side), BF),) * x_size,
            in_specs=[hbm(), hbm(), hbm(), vm(), vm()], out_specs=(vm(),) * x_size,
            scratch_shapes=[
                pltpu.VMEM(act.shape, BF), pltpu.VMEM(bins_shape, F32), pltpu.VMEM((2, cols, tok, side), BF),
                *index_scratch, dma(2), dma(PARTS),
            ],
            compiler_params=params(VMEM_BINS), cost_estimate=cost(4 * slots * tok * side * side, 6 * 2**20), name="bins",
        )(block_rows, block_cols, act, both, got)
        by_x = [pieces[0]]
        for d in range(1, x_size):
            by_x.append(lax.ppermute(pieces[d], "dp", [(p, (p + d * z_size) % n_dp) for p in range(n_dp)]))

        own = pl.pallas_call(
            rows_kernel, out_shape=sds((rows, width), BF), in_specs=[vm()], out_specs=vm(), compiler_params=params(),
            cost_estimate=cost(2**20, 2 * 2**20), name="rows",
        )(parts)
        near = [0, x_size // 2]
        own, *tied = lax.optimization_barrier((own, *(by_x[d] for d in near)))
        for d, v in zip(near, tied):
            by_x[d] = v
        in_grad = lax.all_gather(own, "tensor", axis=0, tiled=True)
        in_grad = pl.pallas_call(
            place_kernel, out_shape=sds((tok, width), BF), in_specs=[hbm()], out_specs=hbm(),
            scratch_shapes=[pltpu.VMEM((tok, width), BF), dma(PARTS), dma(PARTS)],
            compiler_params=params(VMEM_FULL), cost_estimate=cost(0, 4 * 2**20), name="place",
        )(in_grad)

        stage = pl.pallas_call(
            stage_kernel, grid=(4,), out_shape=sds(by_x[0].shape, BF),
            in_specs=[pl.BlockSpec((z_size // 4, 2 * slots * per, side), lambda i: (i, 0, 0))] * x_size,
            out_specs=pl.BlockSpec((z_size // 4, 2 * slots * per, side), lambda i: (i, 0, 0)),
            compiler_params=params(), cost_estimate=cost(2**20, 2 * 2**20), name="stage",
        )(*by_x)
        sums = lax.all_to_all(stage, "dp", 0, 0, axis_index_groups=z_groups, tiled=True)
        win_grad, wout_grad = pl.pallas_call(
            lambda *refs: finish_kernel(bin_scale, *refs),
            out_shape=(sds((slots, per * side), F32), sds((slots, per * side), F32)),
            in_specs=[vm()], out_specs=(vm(), vm()),
            scratch_shapes=[pltpu.VMEM((2 * slots * per, side), F32)], compiler_params=params(), name="finish",
        )(sums)
        return in_grad, win_grad, wout_grad

    return local


def solution(mesh):
    z_size = 8
    in_specs = (
        P("dp", "tensor"),
        P("dp", "tensor"),
        P("tensor", None, None),
        P("tensor", None, None),
        P("tensor", None),
        P("tensor", None),
    )
    out_specs = (P("dp", None), P("tensor", "dp"), P("tensor", "dp"))
    return jax.shard_map(make_local(z_size), mesh=mesh, in_specs=in_specs, out_specs=out_specs, check_vma=False)
```
